256 devices in a mesh: cand: 32 (over y_lo, z, core), img: 8 (over y_hi, x).
Axes of the slice: x: 4, y: 4 (y_hi: 2, y_lo: 2; y = y_hi * 2 + y_lo), z: 8, core: 2. Of those that a mesh axis runs over, the one named last changes fastest.
Arguments:
- first_maps: float32 [8, 256, 344], P('img', 'cand'), may hold values from -6 to 6
- layer_of: int32 [32], P('cand'), may hold values from 0 to 1, as said below
- expand_half: int32 [32], P('cand'), may hold values from 1 to 2
- radius: int32 [32], P('cand'), may hold values from 1 to 2
- teach_up: bfloat16 [2, 344, 2064], replicated, may hold values from -0.3125 to 0.3125
- teach_dw: float32 [2, 25, 2064], replicated, may hold values from -1.25 to 1.25
- teach_down: bfloat16 [2, 344, 2064], replicated, may hold values from -0.125 to 0.125
- cand_up: bfloat16 [32, 344, 2064], P('cand'), may hold values from -0.3125 to 0.3125
- cand_dw: float32 [32, 25, 2064], P('cand'), may hold values from -1.25 to 1.25
- cand_down: bfloat16 [32, 344, 2064], P('cand'), may hold values from -0.125 to 0.125
Outputs:
- grad_up: float32 [32, 344, 2064], P('cand', None, 'img')
- grad_dw: float32 [32, 25, 2064], P('cand', None, 'img')
- grad_down: float32 [32, 344, 2064], P('cand', None, 'img')
The draws below stay inside these ranges and needn't reach their ends.
Inputs may be any that keep to these rules, and one draw needn't show every extreme that they name: `layer_of`: both layers have at least one candidate.
All inputs are finite; a program needn't handle non-finite values.
Results may differ from the reference program's by a relative error of at most 0.014.
Values may be sent and summed in bfloat16 or wider, within the bound.
A program may use at most 192 MiB of HBM per device.

```python
import jax
import jax.numpy as jnp
from jax import lax

C = 344
HID = 2064
H = 16
CELLS = 256
IMG_DEV = 1
IMAGES = 8
CANDIDATES = 32
N_IMG = 8


def draw_layer_of(key, part):
    first_key, second_key = jax.random.split(jax.random.fold_in(key, 17))
    count = jax.random.randint(first_key, (), CANDIDATES // 4, CANDIDATES - CANDIDATES // 4 + 1)
    order = jax.random.permutation(second_key, CANDIDATES)
    return (order >= count).astype(jnp.int32)


def with_ends(values, own_key, smallest, largest):
    place = [jax.random.randint(jax.random.fold_in(own_key, axis), (), 0, length) for axis, length in enumerate(values.shape)]
    main_axis = values.shape.index(max(values.shape))
    neighbour = place[:main_axis] + [(place[main_axis] + 1) % values.shape[main_axis]] + place[main_axis + 1:]
    return values.at[tuple(place)].set(smallest).at[tuple(neighbour)].set(largest)


def block_scale(rng, shape, shards, low, largest):
    loudness = 1.0
    for position, shards_of in shards:
        heights = jax.random.uniform(jax.random.fold_in(jax.random.fold_in(rng, 6), position), (shards_of,), jnp.float32, low / len(shards), largest / len(shards))
        loudness = loudness * jnp.repeat(jnp.exp(heights), shape[position] // shards_of).reshape((-1,) + (1,) * (len(shape) - 1 - position))
    return loudness


def noise(rng, shape, deviation, bound, shards=(), kind=jnp.bfloat16):
    values = deviation * jax.random.normal(rng, shape, jnp.float32)
    if shards:
        values = values * block_scale(rng, shape, shards, -0.22, 0.18)
    return jnp.clip(values, -bound, bound).astype(kind)


def setup_inputs(seed: int = 0) -> dict:
    keys = jax.random.split(jax.random.key(seed), 11)
    return {
        "first_maps": noise(keys[0], (IMAGES, CELLS, C), 1.0, 6.0, ((0, 8), (1, 32)), jnp.float32),
        "layer_of": draw_layer_of(jax.random.fold_in(keys[10], 71), 0),
        "expand_half": with_ends(jax.random.randint(keys[2], (CANDIDATES,), 1, 3), jax.random.fold_in(keys[2], 1), 1, 2).astype(jnp.int32),
        "radius": with_ends(jax.random.randint(keys[3], (CANDIDATES,), 1, 3), jax.random.fold_in(keys[3], 1), 1, 2).astype(jnp.int32),
        "teach_up": noise(keys[4], (2, C, HID), C ** -0.5, 0.3125),
        "teach_dw": noise(keys[5], (2, 25, HID), 25 ** -0.5, 1.25, (), jnp.float32),
        "teach_down": noise(keys[6], (2, C, HID), HID ** -0.5, 0.125),
        "cand_up": noise(keys[7], (CANDIDATES, C, HID), C ** -0.5, 0.3125, ((0, 32),)),
        "cand_dw": noise(keys[8], (CANDIDATES, 25, HID), 25 ** -0.5, 1.25, ((0, 32),), jnp.float32),
        "cand_down": noise(keys[9], (CANDIDATES, C, HID), HID ** -0.5, 0.125, ((0, 32),)),
    }


def apply_block(map_in, w_up, w_dw, w_down, unit_mask, tap_mask):
    batch_size = map_in.shape[0]
    flat_rows = map_in.reshape(-1, map_in.shape[2]).astype(jnp.bfloat16)
    preact = jnp.dot(flat_rows, w_up, preferred_element_type=jnp.float32)
    expanded = jax.nn.silu(preact) * unit_mask
    grid_maps = expanded.reshape(batch_size, H, H, expanded.shape[1])
    padded = jnp.pad(grid_maps, ((0, 0), (2, 2), (2, 2), (0, 0)))
    tap_weights = w_dw * tap_mask[:, None]
    accumulated = jnp.zeros_like(grid_maps)
    for tap_row in range(5):
        for tap_col in range(5):
            accumulated = accumulated + tap_weights[tap_row * 5 + tap_col] * padded[:, tap_row:tap_row + H, tap_col:tap_col + H, :]
    activated = jax.nn.silu(accumulated).reshape(-1, grid_maps.shape[3]).astype(jnp.bfloat16)
    branch = lax.dot_general(activated, w_down, (((1,), (1,)), ((), ())), preferred_element_type=jnp.float32)
    return map_in + branch.reshape(map_in.shape)

def make_masks(half_count, kernel_radius):
    unit_index = lax.broadcasted_iota(jnp.int32, (HID,), 0)
    unit_mask = (unit_index < half_count * (HID // 2)).astype(jnp.float32)
    tap_index = lax.broadcasted_iota(jnp.int32, (25,), 0)
    shift_row = tap_index // 5 - 2
    shift_col = tap_index % 5 - 2
    tap_mask = (jnp.maximum(jnp.abs(shift_row), jnp.abs(shift_col)) <= kernel_radius).astype(jnp.float32)
    return (unit_mask, tap_mask)

def candidate_grads(inputs, target, w_up, w_dw, w_down, unit_mask, tap_mask, images):

    def squared_loss(up_wide, depth_weights, down_wide):
        result = apply_block(inputs, up_wide.astype(jnp.bfloat16), depth_weights, down_wide.astype(jnp.bfloat16), unit_mask, tap_mask)
        error_map = result - target
        return 0.5 * jnp.sum(error_map * error_map) / images
    return jax.grad(squared_loss, argnums=(0, 1, 2))(w_up.astype(jnp.float32), w_dw, w_down.astype(jnp.float32))

def reference(first_maps, layer_of, expand_half, radius, teach_up, teach_dw, teach_down, cand_up, cand_dw, cand_down):
    full_units = jnp.ones((HID,), jnp.float32)
    all_taps = jnp.ones((25,), jnp.float32)
    maps_one = apply_block(first_maps, teach_up[0], teach_dw[0], teach_down[0], full_units, all_taps)
    maps_two = apply_block(maps_one, teach_up[1], teach_dw[1], teach_down[1], full_units, all_taps)

    def one_candidate(cand_index):
        layer_here = layer_of[cand_index]
        inputs = jnp.where(layer_here == 0, first_maps, maps_one)
        target = jnp.where(layer_here == 0, maps_one, maps_two)
        unit_mask, tap_mask = make_masks(expand_half[cand_index], radius[cand_index])

        def one_shard(running, shard_index):
            start = (shard_index * IMG_DEV).astype(jnp.int32)
            part_in = lax.dynamic_slice_in_dim(inputs, start, IMG_DEV, 0)
            part_target = lax.dynamic_slice_in_dim(target, start, IMG_DEV, 0)
            gradients = candidate_grads(part_in, part_target, cand_up[cand_index], cand_dw[cand_index], cand_down[cand_index], unit_mask, tap_mask, IMAGES)
            rounded = tuple((lax.optimization_barrier(piece.astype(jnp.bfloat16)).astype(jnp.float32) for piece in gradients))
            return (tuple((acc + piece for acc, piece in zip(running, rounded))), 0)
        zero_grads = (jnp.zeros((C, HID), jnp.float32), jnp.zeros((25, HID), jnp.float32), jnp.zeros((C, HID), jnp.float32))
        totals, unused = lax.scan(one_shard, zero_grads, jnp.arange(N_IMG, dtype=jnp.int32))
        return totals
    grad_up, grad_dw, grad_down = lax.map(one_candidate, jnp.arange(CANDIDATES, dtype=jnp.int32))
    return (grad_up, grad_dw, grad_down)
```

```python
import functools

import jax
import jax.numpy as jnp
from jax import lax
from jax.experimental import pallas as pl
from jax.experimental.pallas import tpu as pltpu
from jax.sharding import PartitionSpec as P

C = 344
HID = 2064
H = 16
CELLS = 256
CHUNK = 256
FULL = HID // CHUNK
REST = HID - FULL * CHUNK
TILES = 2 * FULL + 1
INNER = (6, 7, 8, 11, 12, 13, 16, 17, 18)
F32 = jnp.float32
BF16 = jnp.bfloat16
MESH = pl.DeviceIdType.MESH


def sigmoid(v):
    return 0.5 * jnp.tanh(0.5 * v) + 0.5


def shift_columns(grid, b, col):
    if b == 0:
        return grid
    flat = pltpu.roll(grid.reshape(CELLS, 128), (-b) % CELLS, 0)
    moved = flat.reshape(H, H, 128)
    keep = col < H - b if b > 0 else col >= -b
    return jnp.where(keep, moved, 0.0)


def depthwise(e, tap):
    col = lax.broadcasted_iota(jnp.int32, (H, H, 128), 1)
    grid = e.reshape(H, H, 128)
    zero = jnp.zeros((2, H, 128), F32)
    total = None
    for b in range(-2, 3):
        moved = jnp.concatenate([zero, shift_columns(grid, b, col), zero], 0)
        for a in range(5):
            term = tap(5 * a + b + 2)[None, None, :] * moved[a : a + H]
            total = term if total is None else total + term
    return total.reshape(CELLS, 128)


def kernel(
    n_cand,
    n_img,
    x_ref,
    layer_ref,
    expand_ref,
    radius_ref,
    tu_hbm,
    tk_hbm,
    td_hbm,
    cu_hbm,
    ck_hbm,
    cd_hbm,
    gu_ref,
    gk_ref,
    gd_ref,
    tu,
    tk,
    td,
    cu,
    ck,
    cd,
    left_u,
    left_d,
    left_k,
    xg,
    x0,
    xb,
    xt,
    acc,
    acc2,
    eb,
    ebt,
    e_s,
    sp_s,
    sk_s,
    g_s,
    p_s,
    rows,
    kg,
    send_d,
    send_u,
    send_h,
    recv_d,
    recv_u,
    recv_h,
    w_sem,
    xs_sem,
    xr_sem,
    ss_sem,
    rs_sem,
):
    me_c = lax.axis_index("cand")
    me_i = lax.axis_index("img")

    copies = []
    for layer in range(2):
        for src, dst in ((tu_hbm, tu), (tk_hbm, tk), (td_hbm, td)):
            copies.append(pltpu.make_async_copy(src.at[layer], dst.at[layer], w_sem.at[len(copies)]))
    for src, dst in ((cu_hbm, cu), (ck_hbm, ck), (cd_hbm, cd)):
        copies.append(pltpu.make_async_copy(src.at[0], dst, w_sem.at[len(copies)]))
    for copy in copies:
        copy.start()

    barrier = pltpu.get_barrier_semaphore()

    def greet_cand(k, carry):
        peer = lax.rem(me_c + k, n_cand)
        pl.semaphore_signal(barrier, inc=1, device_id={"cand": peer}, device_id_type=MESH)
        return carry

    def greet_img(k, carry):
        peer = lax.rem(me_i + k, n_img)
        pl.semaphore_signal(barrier, inc=1, device_id={"img": peer}, device_id_type=MESH)
        return carry

    lax.fori_loop(1, n_cand, greet_cand, 0)
    lax.fori_loop(1, n_img, greet_img, 0)
    pl.semaphore_wait(barrier, n_cand + n_img - 2)

    def map_copy(k):
        peer = lax.rem(me_c + k, n_cand)
        return pltpu.make_async_remote_copy(
            src_ref=x_ref,
            dst_ref=xg.at[me_c],
            send_sem=xs_sem.at[k],
            recv_sem=xr_sem.at[me_c],
            device_id={"cand": peer},
            device_id_type=MESH,
        )

    def map_arrival(k):
        source = lax.rem(me_c + k, n_cand)
        return pltpu.make_async_remote_copy(
            src_ref=x_ref,
            dst_ref=xg.at[source],
            send_sem=xs_sem.at[k],
            recv_sem=xr_sem.at[source],
            device_id={"cand": source},
            device_id_type=MESH,
        )

    def start_map(k, carry):
        map_copy(k).start()
        return carry

    def wait_map(k, carry):
        map_arrival(k).wait_recv()
        return carry

    def wait_sent(k, carry):
        map_copy(k).wait_send()
        return carry

    lax.fori_loop(1, n_cand, start_map, 0)
    xg[me_c] = x_ref[...]

    rows[...] = jnp.zeros_like(rows)
    kg[...] = jnp.zeros_like(kg)
    left_u[...] = jnp.zeros_like(left_u)
    left_d[...] = jnp.zeros_like(left_d)
    left_k[...] = jnp.zeros_like(left_k)

    layer_here = layer_ref[0]
    units_used = expand_ref[0] * (HID // 2)
    outer = jnp.where(radius_ref[0] >= 2, 1.0, 0.0).astype(F32)

    def tap_mask(shape):
        row = lax.broadcasted_iota(jnp.int32, shape, 0)
        inner = row == INNER[0]
        for other in INNER[1:]:
            inner = inner | (row == other)
        return jnp.where(inner, 1.0, outer)

    def unit_mask(tile):
        lane = lax.broadcasted_iota(jnp.int32, (1, 128), 1) + tile * 128
        return jnp.where(lane < units_used, 1.0, 0.0)

    def lanes(j):
        return pl.ds(pl.multiple_of(j * CHUNK, CHUNK), CHUNK)

    def tile_lanes(tile):
        return pl.ds(pl.multiple_of(tile * 128, 128), 128)

    def teacher(layer, inputs, total):
        copies[3 * layer].wait()
        copies[3 * layer + 1].wait()
        copies[3 * layer + 2].wait()
        left_u[layer, :, :REST] = tu[layer, :, FULL * CHUNK :]
        left_d[layer, :, :REST] = td[layer, :, FULL * CHUNK :]
        left_k[layer, :25, :REST] = tk[layer, :, FULL * CHUNK :]

        def active(p, tap):
            k = depthwise(p * sigmoid(p), tap)
            return (k * sigmoid(k)).astype(BF16)

        p = jnp.dot(inputs[...], left_u[layer], preferred_element_type=F32)
        g = active(p, lambda i: left_k[layer, i, :])
        total[...] = lax.dot_general(
            g, left_d[layer], (((1,), (1,)), ((), ())), preferred_element_type=F32
        )

        def step(j, carry):
            p_s[...] = jnp.dot(inputs[...], tu[layer, :, lanes(j)], preferred_element_type=F32)
            for half in range(2):
                part = slice(128 * half, 128 * half + 128)
                tile = 2 * j + half
                g_s[FULL, :, part] = active(
                    p_s[:, part], lambda i: tk[layer, i, tile_lanes(tile)]
                )
            total[...] += lax.dot_general(
                g_s[FULL], td[layer, :, lanes(j)], (((1,), (1,)), ((), ())), preferred_element_type=F32
            )
            return carry

        lax.fori_loop(0, FULL, step, 0)

    lax.fori_loop(1, n_cand, wait_map, 0)
    x_wide = xg[...].astype(F32).reshape(CELLS, C)
    x0[...] = x_wide
    xb[...] = x_wide.astype(BF16)
    teacher(0, xb, acc)

    ones = x0[...] + acc[...]
    xb[...] = ones.astype(BF16)
    teacher(1, xb, acc2)
    first = layer_here == 0
    wide = jnp.where(first, x0[...], x0[...] + acc[...])
    xb[...] = wide.astype(BF16)
    acc[...] = jnp.where(first, acc[...], acc2[...])
    pad = jnp.zeros((CELLS, 384 - C), F32)
    xt[...] = jnp.transpose(jnp.concatenate([wide, pad], 1))[:C].astype(BF16)

    for copy in copies[6:]:
        copy.wait()
    ck[...] = ck[...] * tap_mask((25, HID))
    left_u[2, :, :REST] = cu[:, FULL * CHUNK :]
    left_d[2, :, :REST] = cd[:, FULL * CHUNK :]
    left_k[2, :25, :REST] = ck[:, FULL * CHUNK :]

    def forward_tile(p, tile, tap):
        mask = unit_mask(tile)
        s = sigmoid(p) * mask
        e = p * s
        e_s[tile] = e
        sp_s[tile] = s + e * (1.0 - s)
        k = depthwise(e, tap)
        s2 = sigmoid(k)
        g = k * s2
        sk_s[tile] = s2 + g * (1.0 - s2)
        return g.astype(BF16)

    p = jnp.dot(xb[...], left_u[2], preferred_element_type=F32)
    g = forward_tile(p, 2 * FULL, lambda i: left_k[2, i, :])
    g_s[FULL, :, :128] = g
    acc2[...] = lax.dot_general(g, left_d[2], (((1,), (1,)), ((), ())), preferred_element_type=F32)

    def forward(j, carry):
        p_s[...] = jnp.dot(xb[...], cu[:, lanes(j)], preferred_element_type=F32)
        for half in range(2):
            part = slice(128 * half, 128 * half + 128)
            tile = 2 * j + half
            g_s[j, :, part] = forward_tile(
                p_s[:, part], tile, lambda i: ck[i, tile_lanes(tile)]
            )
        acc2[...] += lax.dot_general(
            g_s[j], cd[:, lanes(j)], (((1,), (1,)), ((), ())), preferred_element_type=F32
        )
        return carry

    lax.fori_loop(0, FULL, forward, 0)

    error = (acc2[...] - acc[...]) * (1.0 / n_img)
    eb[...] = error.astype(BF16)
    ebt[...] = jnp.transpose(jnp.concatenate([error, pad], 1))[:C].astype(BF16)

    def grad_copy(kind, peer, slot, source):
        src, dst = ((send_d, recv_d), (send_u, recv_u), (send_h, recv_h))[kind]
        return pltpu.make_async_remote_copy(
            src_ref=src.at[slot],
            dst_ref=dst.at[source],
            send_sem=ss_sem.at[kind, slot],
            recv_sem=rs_sem.at[kind, source],
            device_id={"img": peer},
            device_id_type=MESH,
        )

    def head(block, other):
        turned = jnp.transpose(block)[:REST].astype(BF16)
        return jnp.dot(turned, other, preferred_element_type=F32).astype(BF16)

    def down_step(t, carry):
        j = lax.rem(me_i + n_img - t, n_img)
        send_d[j] = jnp.dot(ebt[...], g_s[j], preferred_element_type=F32).astype(BF16)
        before = lax.rem(j + n_img - 1, n_img)

        @pl.when(j > 0)
        def _():
            send_h[before, :REST, :C] = head(g_s[j, :, :128].astype(F32), eb[...])

        @pl.when(t > 0)
        def _():
            grad_copy(0, j, j, me_i).start()

        return carry

    send_h[n_img - 1, :REST, :C] = head(g_s[FULL, :, :128].astype(F32), eb[...])
    lax.fori_loop(0, n_img, down_step, 0)
    recv_d[me_i] = send_d[me_i]

    def backward_tile(dg, tile, tap):
        col = lax.broadcasted_iota(jnp.int32, (H, H, 128), 1)
        grid = (dg * sk_s[tile]).reshape(H, H, 128)
        for b in range(-2, 3):
            rows[b + 2, 2 : 2 + H] = shift_columns(grid, -b, col)
        total = [None] * H
        for b in range(-2, 3):
            sums = [None] * 5
            for r in range(H):
                e = e_s[tile, H * r : H * r + H, :]
                for a in range(-2, 3):
                    moved = rows[b + 2, 2 - a + r]
                    term = tap(5 * (a + 2) + b + 2)[None, :] * moved
                    total[r] = term if total[r] is None else total[r] + term
                    q = moved * e
                    q = q[:8] + q[8:]
                    sums[a + 2] = q if sums[a + 2] is None else sums[a + 2] + q
            for a in range(5):
                kg[5 * a + b + 2, :] = jnp.sum(sums[a], axis=0)
        de = jnp.concatenate(total, 0)
        return de * sp_s[tile]

    taps = tap_mask((32, 128))

    dg = jnp.dot(eb[...], left_d[2], preferred_element_type=F32)
    dp = backward_tile(dg, 2 * FULL, lambda i: left_k[2, i, :])
    send_h[n_img - 1, REST : 2 * REST, :C] = head(dp, xb[...])
    send_h[n_img - 1, 32:64, 256:384] = (kg[...] * taps).astype(BF16)

    def up_step(t, carry):
        j = lax.rem(me_i + n_img - t, n_img)
        before = lax.rem(j + n_img - 1, n_img)
        p_s[...] = jnp.dot(eb[...], cd[:, lanes(j)], preferred_element_type=F32)
        for half in range(2):
            part = slice(128 * half, 128 * half + 128)
            tile = 2 * j + half
            dp = backward_tile(p_s[:, part], tile, lambda i: ck[i, tile_lanes(tile)])
            dk = (kg[...] * taps).astype(BF16)
            send_h[j, 32:64, part] = dk
            p_s[:, part] = dp
            if half == 0:

                @pl.when(j > 0)
                def _():
                    send_h[before, REST : 2 * REST, :C] = head(p_s[:, :128], xb[...])
                    send_h[before, 32:64, 256:384] = dk

        send_u[j] = jnp.dot(xt[...], p_s[...].astype(BF16), preferred_element_type=F32).astype(BF16)

        @pl.when(t > 0)
        def _():
            grad_copy(1, j, j, me_i).start()
            grad_copy(2, j, j, me_i).start()

        return carry

    lax.fori_loop(0, n_img, up_step, 0)
    recv_u[me_i] = send_u[me_i]
    recv_h[me_i] = send_h[me_i]

    def arrivals(k, carry):
        source = lax.rem(me_i + k, n_img)
        for kind in range(3):
            grad_copy(kind, source, source, source).wait_recv()
        return carry

    lax.fori_loop(1, n_img, arrivals, 0)

    heads = recv_h[0].astype(F32)
    for source in range(1, n_img):
        heads = heads + recv_h[source].astype(F32)
    amount = lax.rem(384 - 2 * me_i, 384)
    wide_zero = jnp.zeros((128 - REST, 384), F32)

    def assemble(recv, head_rows, out):
        main = recv[0].astype(F32)
        for source in range(1, n_img):
            main = main + recv[source].astype(F32)
        tail = jnp.transpose(jnp.concatenate([head_rows, wide_zero], 0))[:C]
        whole = pltpu.roll(jnp.concatenate([main, tail], 1), amount, 1)
        out[...] = whole[:, : CHUNK + 2]

    assemble(recv_d, heads[:REST], gd_ref)
    assemble(recv_u, heads[REST : 2 * REST], gu_ref)
    gk_ref[...] = pltpu.roll(heads[32:64], amount, 1)[:25, : CHUNK + 2]

    lax.fori_loop(1, n_cand, wait_sent, 0)

    def sent(k, carry):
        peer = lax.rem(me_i + k, n_img)
        for kind in range(3):
            grad_copy(kind, peer, peer, me_i).wait_send()
        return carry

    lax.fori_loop(1, n_img, sent, 0)


def body(n_cand, n_img, first_maps, layer_of, expand_half, radius, *weights):
    teach_up, teach_dw, teach_down, cand_up, cand_dw, cand_down = weights
    vmem = pl.BlockSpec(memory_space=pltpu.VMEM)
    smem = pl.BlockSpec(memory_space=pltpu.SMEM)
    hbm = pl.BlockSpec(memory_space=pl.ANY)
    own = CHUNK + 2
    grads = pl.pallas_call(
        functools.partial(kernel, n_cand, n_img),
        out_shape=(
            jax.ShapeDtypeStruct((C, own), F32),
            jax.ShapeDtypeStruct((25, own), F32),
            jax.ShapeDtypeStruct((C, own), F32),
        ),
        in_specs=[vmem, smem, smem, smem] + [hbm] * 6,
        out_specs=(vmem, vmem, vmem),
        scratch_shapes=[
            pltpu.VMEM((2, C, HID), BF16),
            pltpu.VMEM((2, 25, HID), F32),
            pltpu.VMEM((2, C, HID), BF16),
            pltpu.VMEM((C, HID), BF16),
            pltpu.VMEM((25, HID), F32),
            pltpu.VMEM((C, HID), BF16),
            pltpu.VMEM((3, C, 128), BF16),
            pltpu.VMEM((3, C, 128), BF16),
            pltpu.VMEM((3, 32, 128), F32),
            pltpu.VMEM((n_cand, 8, C), BF16),
            pltpu.VMEM((CELLS, C), F32),
            pltpu.VMEM((CELLS, C), BF16),
            pltpu.VMEM((C, CELLS), BF16),
            pltpu.VMEM((CELLS, C), F32),
            pltpu.VMEM((CELLS, C), F32),
            pltpu.VMEM((CELLS, C), BF16),
            pltpu.VMEM((C, CELLS), BF16),
            pltpu.VMEM((TILES, CELLS, 128), F32),
            pltpu.VMEM((TILES, CELLS, 128), F32),
            pltpu.VMEM((TILES, CELLS, 128), F32),
            pltpu.VMEM((FULL + 1, CELLS, CHUNK), BF16),
            pltpu.VMEM((CELLS, CHUNK), F32),
            pltpu.VMEM((5, H + 4, H, 128), F32),
            pltpu.VMEM((32, 128), F32),
            pltpu.VMEM((n_img, C, CHUNK), BF16),
            pltpu.VMEM((n_img, C, CHUNK), BF16),
            pltpu.VMEM((n_img, 64, 384), BF16),
            pltpu.VMEM((n_img, C, CHUNK), BF16),
            pltpu.VMEM((n_img, C, CHUNK), BF16),
            pltpu.VMEM((n_img, 64, 384), BF16),
            pltpu.SemaphoreType.DMA((9,)),
            pltpu.SemaphoreType.DMA((n_cand,)),
            pltpu.SemaphoreType.DMA((n_cand,)),
            pltpu.SemaphoreType.DMA((3, n_img)),
            pltpu.SemaphoreType.DMA((3, n_img)),
        ],
        compiler_params=pltpu.CompilerParams(
            collective_id=0, has_side_effects=True, vmem_limit_bytes=56 * 1024 * 1024
        ),
        name="step",
    )(
        first_maps[0].astype(BF16),
        layer_of,
        expand_half,
        radius,
        teach_up,
        teach_dw,
        teach_down,
        cand_up,
        cand_dw,
        cand_down,
    )
    return tuple(grad[None] for grad in grads)


def solution(mesh):
    placed = (
        P("img", "cand", None),
        P("cand"),
        P("cand"),
        P("cand"),
        P(),
        P(),
        P(),
        P("cand", None, None),
        P("cand", None, None),
        P("cand", None, None),
    )
    return jax.shard_map(
        functools.partial(body, mesh.shape["cand"], mesh.shape["img"]),
        mesh=mesh,
        in_specs=placed,
        out_specs=(P("cand", None, "img"), P("cand", None, "img"), P("cand", None, "img")),
        check_vma=False,
    )
```

```python
import functools

import jax
import jax.numpy as jnp
from jax import lax
from jax.experimental import pallas as pl
from jax.experimental.pallas import tpu as pltpu
from jax.sharding import PartitionSpec as P

C = 344
HID = 2064
H = 16
CELLS = 256
CHUNK = 256
FULL = HID // CHUNK
REST = HID - FULL * CHUNK
TILES = 2 * FULL + 1
INNER = (6, 7, 8, 11, 12, 13, 16, 17, 18)
F32 = jnp.float32
BF16 = jnp.bfloat16
MESH = pl.DeviceIdType.MESH


def sigmoid(v):
    return 0.5 * jnp.tanh(0.5 * v) + 0.5


def shift_columns(grid, b, col):
    if b == 0:
        return grid
    flat = pltpu.roll(grid.reshape(CELLS, 128), (-b) % CELLS, 0)
    moved = flat.reshape(H, H, 128)
    keep = col < H - b if b > 0 else col >= -b
    return jnp.where(keep, moved, 0.0)


def depthwise(e, tap):
    col = lax.broadcasted_iota(jnp.int32, (H, H, 128), 1)
    grid = e.reshape(H, H, 128)
    zero = jnp.zeros((2, H, 128), F32)
    total = None
    for b in range(-2, 3):
        moved = jnp.concatenate([zero, shift_columns(grid, b, col), zero], 0)
        for a in range(5):
            term = tap(5 * a + b + 2)[None, None, :] * moved[a : a + H]
            total = term if total is None else total + term
    return total.reshape(CELLS, 128)


def depthwise_row(e, tap):
    col = lax.broadcasted_iota(jnp.int32, (5, H, 128), 1)
    total = None
    for b in range(-2, 3):
        if b == 0:
            moved = e.reshape(5, H, 128)
        else:
            moved = pltpu.roll(e, (-b) % (5 * H), 0).reshape(5, H, 128)
            moved = jnp.where(col < H - b if b > 0 else col >= -b, moved, 0.0)
        for a in range(5):
            term = tap(5 * a + b + 2)[None, :] * moved[a]
            total = term if total is None else total + term
    return total


def finish(gu_ref, gk_ref, gd_ref, up_ref, dw_ref, down_ref):
    own = CHUNK + 2
    for src, dst in ((gu_ref, up_ref), (gd_ref, down_ref)):
        dst[:, 0, :] = jnp.transpose(src[...])[:own, :C]
    dw_ref[:, 0, :] = gk_ref[:25, :own]


def kernel(
    n_cand,
    n_img,
    x_ref,
    layer_ref,
    expand_ref,
    radius_ref,
    tu_hbm,
    tk_hbm,
    td_hbm,
    cu_hbm,
    ck_hbm,
    cd_hbm,
    gu_ref,
    gk_ref,
    gd_ref,
    tu,
    tk,
    td,
    cu,
    ck,
    cd,
    left_u,
    left_d,
    left_k,
    xg,
    x0,
    xb,
    xt,
    acc,
    acc2,
    eb,
    ebt,
    e_s,
    sp_s,
    sk_s,
    g_s,
    p_s,
    rows,
    kg,
    send_d,
    send_u,
    send_h,
    recv_d,
    recv_u,
    recv_h,
    w_sem,
    xs_sem,
    xr_sem,
    ss_sem,
    rs_sem,
    base,
    xpad,
    xh,
    row_out,
    row_in,
    pair_sem,
    ts_sem,
    tr_sem,
):
    me_c = lax.axis_index("cand")
    me_i = lax.axis_index("img")

    copies = []
    for layer in range(2):
        for src, dst in ((tu_hbm, tu), (td_hbm, td)):
            copies.append(pltpu.make_async_copy(src.at[layer], dst.at[layer], w_sem.at[len(copies)]))
    copies.insert(0, pltpu.make_async_copy(tk_hbm, tk, w_sem.at[len(copies)]))
    for src, dst in ((cu_hbm.at[0], cu), (ck_hbm, ck), (cd_hbm.at[0], cd)):
        copies.append(pltpu.make_async_copy(src, dst, w_sem.at[len(copies)]))
    for copy in copies:
        copy.start()

    xh[...] = x_ref[0].astype(BF16)
    barrier = pltpu.get_barrier_semaphore()

    def greet_cand(k, carry):
        peer = lax.rem(me_c + k, n_cand)
        pl.semaphore_signal(barrier, inc=1, device_id={"cand": peer}, device_id_type=MESH)
        return carry

    def greet_img(k, carry):
        peer = lax.rem(me_i + k, n_img)
        pl.semaphore_signal(barrier, inc=1, device_id={"img": peer}, device_id_type=MESH)
        return carry

    lax.fori_loop(1, n_cand, greet_cand, 0)
    lax.fori_loop(1, n_img, greet_img, 0)
    pl.semaphore_wait(barrier, n_cand + n_img - 2)

    def map_copy(k):
        peer = lax.rem(me_c + k, n_cand)
        return pltpu.make_async_remote_copy(
            src_ref=xh,
            dst_ref=xg.at[me_c],
            send_sem=xs_sem.at[k],
            recv_sem=xr_sem.at[me_c],
            device_id={"cand": peer},
            device_id_type=MESH,
        )

    def map_arrival(k):
        source = lax.rem(me_c + k, n_cand)
        return pltpu.make_async_remote_copy(
            src_ref=xh,
            dst_ref=xg.at[source],
            send_sem=xs_sem.at[k],
            recv_sem=xr_sem.at[source],
            device_id={"cand": source},
            device_id_type=MESH,
        )

    def start_map(k, carry):
        map_copy(k).start()
        return carry

    def wait_map(k, carry):
        map_arrival(k).wait_recv()
        return carry

    def wait_sent(k, carry):
        map_copy(k).wait_send()
        return carry

    lax.fori_loop(1, n_cand, start_map, 0)
    xg[me_c] = xh[...]

    rows[...] = jnp.zeros_like(rows)
    xpad[...] = jnp.zeros_like(xpad)
    kg[...] = jnp.zeros_like(kg)
    left_u[...] = jnp.zeros_like(left_u)
    left_d[...] = jnp.zeros_like(left_d)
    left_k[...] = jnp.zeros_like(left_k)

    layer_here = layer_ref[0]
    units_used = expand_ref[0] * (HID // 2)
    outer = jnp.where(radius_ref[0] >= 2, 1.0, 0.0).astype(F32)

    def tap_mask(shape):
        row = lax.broadcasted_iota(jnp.int32, shape, 0)
        inner = row == INNER[0]
        for other in INNER[1:]:
            inner = inner | (row == other)
        return jnp.where(inner, 1.0, outer)

    def unit_mask(tile):
        lane = lax.broadcasted_iota(jnp.int32, (1, 128), 1) + tile * 128
        return jnp.where(lane < units_used, 1.0, 0.0)

    def lanes(j):
        return pl.ds(pl.multiple_of(j * CHUNK, CHUNK), CHUNK)

    def tile_lanes(tile):
        return pl.ds(pl.multiple_of(tile * 128, 128), 128)

    def active(p, conv):
        k = conv(p * sigmoid(p))
        return (k * sigmoid(k)).astype(BF16)

    def whole_map(tap):
        return lambda e: depthwise(e, tap)

    def one_row(tap):
        return lambda e: depthwise_row(e, tap)

    def load_left(layer):
        left_u[layer, :, :REST] = tu[layer, :, FULL * CHUNK :]
        left_d[layer, :, :REST] = td[layer, :, FULL * CHUNK :]
        left_k[layer, :25, :REST] = tk[:, layer, FULL * CHUNK :]

    core = lax.rem(me_c, 2)
    map_row = me_c // 2

    def teacher_first():
        for copy in copies[:3]:
            copy.wait()
        load_left(0)
        p = jnp.dot(xb[...], left_u[0], preferred_element_type=F32)
        g = active(p, whole_map(lambda i: left_k[0, i, :]))
        rest = lax.dot_general(g, left_d[0], (((1,), (1,)), ((), ())), preferred_element_type=F32)
        acc[...] = jnp.where(core == 0, rest, 0.0)

        def step(t, carry):
            j = core * (FULL // 2) + t
            p_s[...] = jnp.dot(xb[...], tu[0, :, lanes(j)], preferred_element_type=F32)
            for half in range(2):
                part = slice(128 * half, 128 * half + 128)
                tile = 2 * j + half
                g_s[FULL, :, part] = active(
                    p_s[:, part], whole_map(lambda i: tk[i, 0, tile_lanes(tile)])
                )
            acc[...] += lax.dot_general(
                g_s[FULL], td[0, :, lanes(j)], (((1,), (1,)), ((), ())), preferred_element_type=F32
            )
            return carry

        lax.fori_loop(0, FULL // 2, step, 0)

    def pair_copy():
        return pltpu.make_async_remote_copy(
            src_ref=acc,
            dst_ref=acc2,
            send_sem=pair_sem.at[0],
            recv_sem=pair_sem.at[1],
            device_id={"cand": me_c + 1 - 2 * core},
            device_id_type=MESH,
        )

    def teacher_row():
        for copy in copies[3:5]:
            copy.wait()
        load_left(1)
        near = xpad[pl.ds(pl.multiple_of(map_row * H, H), 5 * H), :]
        p = jnp.dot(near, left_u[1], preferred_element_type=F32)
        g = active(p, one_row(lambda i: left_k[1, i, :]))
        rest = lax.dot_general(g, left_d[1], (((1,), (1,)), ((), ())), preferred_element_type=F32)

        def step(j, total):
            p = jnp.dot(
                xpad[pl.ds(pl.multiple_of(map_row * H, H), 5 * H), :],
                tu[1, :, lanes(j)],
                preferred_element_type=F32,
            )
            parts = []
            for half in range(2):
                tile = 2 * j + half
                parts.append(
                    active(
                        p[:, 128 * half : 128 * half + 128],
                        one_row(lambda i: tk[i, 1, tile_lanes(tile)]),
                    )
                )
            return total + lax.dot_general(
                jnp.concatenate(parts, 1),
                td[1, :, lanes(j)],
                (((1,), (1,)), ((), ())),
                preferred_element_type=F32,
            )

        row_out[...] = lax.fori_loop(0, FULL, step, rest).astype(BF16)

    def row_copy(k):
        peer = lax.rem(me_c + 2 * k, n_cand)
        return pltpu.make_async_remote_copy(
            src_ref=row_out,
            dst_ref=row_in.at[map_row],
            send_sem=ts_sem.at[k],
            recv_sem=tr_sem.at[map_row],
            device_id={"cand": peer},
            device_id_type=MESH,
        )

    def row_arrival(k):
        source = lax.rem(map_row + k, H)
        return pltpu.make_async_remote_copy(
            src_ref=row_out,
            dst_ref=row_in.at[source],
            send_sem=ts_sem.at[k],
            recv_sem=tr_sem.at[source],
            device_id={"cand": lax.rem(me_c + 2 * k, n_cand)},
            device_id_type=MESH,
        )

    def start_row(k, carry):
        row_copy(k).start()
        return carry

    def wait_row(k, carry):
        row_arrival(k).wait_recv()
        return carry

    def sent_row(k, carry):
        row_copy(k).wait_send()
        return carry

    lax.fori_loop(1, n_cand, wait_map, 0)
    x_wide = xg[...].astype(F32).reshape(CELLS, C)
    x0[...] = x_wide
    xb[...] = x_wide.astype(BF16)
    teacher_first()
    pair = pair_copy()
    pair.start()
    pair.wait()
    ones = x0[...] + (acc[...] + acc2[...])
    base[...] = acc[...] + acc2[...]
    xpad[2 * H : 2 * H + CELLS] = ones.astype(BF16)
    teacher_row()
    first = layer_here == 0
    wide = jnp.where(first, x0[...], ones)
    xb[...] = wide.astype(BF16)
    pad = jnp.zeros((CELLS, 384 - C), F32)
    xt[...] = jnp.transpose(jnp.concatenate([wide, pad], 1))[:C].astype(BF16)

    for copy in copies[5:]:
        copy.wait()
    ck[...] = ck[...] * tap_mask((25, 1, HID))
    left_u[2, :, :REST] = cu[:, FULL * CHUNK :]
    left_d[2, :, :REST] = cd[:, FULL * CHUNK :]
    left_k[2, :25, :REST] = ck[:, 0, FULL * CHUNK :]

    def forward_tile(p, tile, tap):
        mask = unit_mask(tile)
        s = sigmoid(p) * mask
        e = p * s
        e_s[tile] = e
        sp_s[tile] = s + e * (1.0 - s)
        k = depthwise(e, tap)
        s2 = sigmoid(k)
        g = k * s2
        sk_s[tile] = s2 + g * (1.0 - s2)
        return g.astype(BF16)

    p = jnp.dot(xb[...], left_u[2], preferred_element_type=F32)
    g = forward_tile(p, 2 * FULL, lambda i: left_k[2, i, :])
    g_s[FULL, :, :128] = g
    acc2[...] = lax.dot_general(g, left_d[2], (((1,), (1,)), ((), ())), preferred_element_type=F32)

    lax.fori_loop(1, H, start_row, 0)
    row_in[map_row] = row_out[...]

    def forward(j, carry):
        p_s[...] = jnp.dot(xb[...], cu[:, lanes(j)], preferred_element_type=F32)
        for half in range(2):
            part = slice(128 * half, 128 * half + 128)
            tile = 2 * j + half
            g_s[j, :, part] = forward_tile(
                p_s[:, part], tile, lambda i: ck[i, 0, tile_lanes(tile)]
            )
        acc2[...] += lax.dot_general(
            g_s[j], cd[:, lanes(j)], (((1,), (1,)), ((), ())), preferred_element_type=F32
        )
        return carry

    lax.fori_loop(0, FULL, forward, 0)

    lax.fori_loop(1, H, wait_row, 0)
    second = row_in[...].astype(F32).reshape(CELLS, C)
    error = (acc2[...] - jnp.where(first, base[...], second)) * (1.0 / n_img)
    eb[...] = error.astype(BF16)
    ebt[...] = jnp.transpose(jnp.concatenate([error, pad], 1))[:C].astype(BF16)

    def grad_copy(kind, peer, slot, source):
        src, dst = ((send_d, recv_d), (send_u, recv_u), (send_h, recv_h))[kind]
        return pltpu.make_async_remote_copy(
            src_ref=src.at[slot],
            dst_ref=dst.at[source],
            send_sem=ss_sem.at[kind, slot],
            recv_sem=rs_sem.at[kind, source],
            device_id={"img": peer},
            device_id_type=MESH,
        )

    def head(block, other):
        turned = jnp.transpose(block)[:REST].astype(BF16)
        return jnp.dot(turned, other, preferred_element_type=F32).astype(BF16)

    def down_step(t, carry):
        j = lax.rem(me_i + n_img - t, n_img)
        send_d[j] = jnp.dot(ebt[...], g_s[j], preferred_element_type=F32).astype(BF16)
        before = lax.rem(j + n_img - 1, n_img)

        @pl.when(j > 0)
        def _():
            send_h[before, :REST, :C] = head(g_s[j, :, :128].astype(F32), eb[...])

        @pl.when(t > 0)
        def _():
            grad_copy(0, j, j, me_i).start()

        return carry

    send_h[n_img - 1, :REST, :C] = head(g_s[FULL, :, :128].astype(F32), eb[...])
    lax.fori_loop(0, n_img, down_step, 0)
    recv_d[me_i] = send_d[me_i]

    def backward_tile(dg, tile, tap):
        col = lax.broadcasted_iota(jnp.int32, (H, H, 128), 1)
        grid = (dg * sk_s[tile]).reshape(H, H, 128)
        for b in range(-2, 3):
            rows[b + 2, 2 : 2 + H] = shift_columns(grid, -b, col)
        total = [None] * H
        for b in range(-2, 3):
            sums = [None] * 5
            for r in range(H):
                e = e_s[tile, H * r : H * r + H, :]
                for a in range(-2, 3):
                    moved = rows[b + 2, 2 - a + r]
                    term = tap(5 * (a + 2) + b + 2)[None, :] * moved
                    total[r] = term if total[r] is None else total[r] + term
                    q = moved * e
                    q = q[:8] + q[8:]
                    sums[a + 2] = q if sums[a + 2] is None else sums[a + 2] + q
            for a in range(5):
                kg[5 * a + b + 2, :] = jnp.sum(sums[a], axis=0)
        de = jnp.concatenate(total, 0)
        return de * sp_s[tile]

    taps = tap_mask((32, 128))

    dg = jnp.dot(eb[...], left_d[2], preferred_element_type=F32)
    dp = backward_tile(dg, 2 * FULL, lambda i: left_k[2, i, :])
    send_h[n_img - 1, REST : 2 * REST, :C] = head(dp, xb[...])
    send_h[n_img - 1, 32:64, 256:384] = (kg[...] * taps).astype(BF16)

    def up_step(t, carry):
        j = lax.rem(me_i + n_img - t, n_img)
        before = lax.rem(j + n_img - 1, n_img)
        p_s[...] = jnp.dot(eb[...], cd[:, lanes(j)], preferred_element_type=F32)
        for half in range(2):
            part = slice(128 * half, 128 * half + 128)
            tile = 2 * j + half
            dp = backward_tile(p_s[:, part], tile, lambda i: ck[i, 0, tile_lanes(tile)])
            dk = (kg[...] * taps).astype(BF16)
            send_h[j, 32:64, part] = dk
            p_s[:, part] = dp
            if half == 0:

                @pl.when(j > 0)
                def _():
                    send_h[before, REST : 2 * REST, :C] = head(p_s[:, :128], xb[...])
                    send_h[before, 32:64, 256:384] = dk

        send_u[j] = jnp.dot(xt[...], p_s[...].astype(BF16), preferred_element_type=F32).astype(BF16)

        @pl.when(t > 0)
        def _():
            grad_copy(1, j, j, me_i).start()
            grad_copy(2, j, j, me_i).start()

        return carry

    lax.fori_loop(0, n_img, up_step, 0)
    recv_u[me_i] = send_u[me_i]
    recv_h[me_i] = send_h[me_i]

    def arrivals(k, carry):
        source = lax.rem(me_i + k, n_img)
        for kind in range(3):
            grad_copy(kind, source, source, source).wait_recv()
        return carry

    lax.fori_loop(1, n_img, arrivals, 0)

    heads = recv_h[0].astype(F32)
    for source in range(1, n_img):
        heads = heads + recv_h[source].astype(F32)
    amount = lax.rem(384 - 2 * me_i, 384)
    wide_zero = jnp.zeros((128 - REST, 384), F32)

    def assemble(recv, head_rows, out):
        main = recv[0].astype(F32)
        for source in range(1, n_img):
            main = main + recv[source].astype(F32)
        tail = jnp.transpose(jnp.concatenate([head_rows, wide_zero], 0))[:C]
        whole = pltpu.roll(jnp.concatenate([main, tail], 1), amount, 1)
        out[:C, :] = whole
        out[C:, :] = jnp.zeros((384 - C, 384), F32)

    assemble(recv_d, heads[:REST], gd_ref)
    assemble(recv_u, heads[REST : 2 * REST], gu_ref)
    gk_ref[...] = pltpu.roll(heads[32:64], amount, 1)

    lax.fori_loop(1, n_cand, wait_sent, 0)
    lax.fori_loop(1, H, sent_row, 0)

    def sent(k, carry):
        peer = lax.rem(me_i + k, n_img)
        for kind in range(3):
            grad_copy(kind, peer, peer, me_i).wait_send()
        return carry

    lax.fori_loop(1, n_img, sent, 0)


def body(n_cand, n_img, first_maps, layer_of, expand_half, radius, *weights):
    teach_up, teach_dw, teach_down, cand_up, cand_dw, cand_down = weights
    vmem = pl.BlockSpec(memory_space=pltpu.VMEM)
    smem = pl.BlockSpec(memory_space=pltpu.SMEM)
    hbm = pl.BlockSpec(memory_space=pl.ANY)
    own = CHUNK + 2
    grads = pl.pallas_call(
        functools.partial(kernel, n_cand, n_img),
        out_shape=(
            jax.ShapeDtypeStruct((384, 384), F32),
            jax.ShapeDtypeStruct((32, 384), F32),
            jax.ShapeDtypeStruct((384, 384), F32),
        ),
        in_specs=[vmem, smem, smem, smem] + [hbm] * 6,
        out_specs=(vmem, vmem, vmem),
        scratch_shapes=[
            pltpu.VMEM((2, C, HID), BF16),
            pltpu.VMEM((25, 2, HID), F32),
            pltpu.VMEM((2, C, HID), BF16),
            pltpu.VMEM((C, HID), BF16),
            pltpu.VMEM((25, 1, HID), F32),
            pltpu.VMEM((C, HID), BF16),
            pltpu.VMEM((3, C, 128), BF16),
            pltpu.VMEM((3, C, 128), BF16),
            pltpu.VMEM((3, 32, 128), F32),
            pltpu.VMEM((n_cand, 8, C), BF16),
            pltpu.VMEM((CELLS, C), F32),
            pltpu.VMEM((CELLS, C), BF16),
            pltpu.VMEM((C, CELLS), BF16),
            pltpu.VMEM((CELLS, C), F32),
            pltpu.VMEM((CELLS, C), F32),
            pltpu.VMEM((CELLS, C), BF16),
            pltpu.VMEM((C, CELLS), BF16),
            pltpu.VMEM((TILES, CELLS, 128), F32),
            pltpu.VMEM((TILES, CELLS, 128), F32),
            pltpu.VMEM((TILES, CELLS, 128), F32),
            pltpu.VMEM((FULL + 1, CELLS, CHUNK), BF16),
            pltpu.VMEM((CELLS, CHUNK), F32),
            pltpu.VMEM((5, H + 4, H, 128), F32),
            pltpu.VMEM((32, 128), F32),
            pltpu.VMEM((n_img, C, CHUNK), BF16),
            pltpu.VMEM((n_img, C, CHUNK), BF16),
            pltpu.VMEM((n_img, 64, 384), BF16),
            pltpu.VMEM((n_img, C, CHUNK), BF16),
            pltpu.VMEM((n_img, C, CHUNK), BF16),
            pltpu.VMEM((n_img, 64, 384), BF16),
            pltpu.SemaphoreType.DMA((9,)),
            pltpu.SemaphoreType.DMA((n_cand,)),
            pltpu.SemaphoreType.DMA((n_cand,)),
            pltpu.SemaphoreType.DMA((3, n_img)),
            pltpu.SemaphoreType.DMA((3, n_img)),
            pltpu.VMEM((CELLS, C), F32),
            pltpu.VMEM((CELLS + 4 * H, C), BF16),
            pltpu.VMEM((8, C), BF16),
            pltpu.VMEM((H, C), BF16),
            pltpu.VMEM((H, H, C), BF16),
            pltpu.SemaphoreType.DMA((2,)),
            pltpu.SemaphoreType.DMA((H,)),
            pltpu.SemaphoreType.DMA((H,)),
        ],
        compiler_params=pltpu.CompilerParams(
            collective_id=0, has_side_effects=True, vmem_limit_bytes=56 * 1024 * 1024
        ),
        name="step",
    )(
        first_maps,
        layer_of,
        expand_half,
        radius,
        teach_up,
        jnp.transpose(teach_dw, (1, 0, 2)),
        teach_down,
        cand_up,
        jnp.transpose(cand_dw, (1, 0, 2)),
        cand_down,
    )
    up, dw, down = pl.pallas_call(
        finish,
        out_shape=(
            jax.ShapeDtypeStruct((own, 1, C), F32),
            jax.ShapeDtypeStruct((25, 1, own), F32),
            jax.ShapeDtypeStruct((own, 1, C), F32),
        ),
        in_specs=[vmem] * 3,
        out_specs=(vmem, vmem, vmem),
        compiler_params=pltpu.CompilerParams(vmem_limit_bytes=8 * 1024 * 1024),
        name="finish",
    )(*grads)
    return (
        jnp.transpose(up, (1, 2, 0)),
        jnp.transpose(dw, (1, 0, 2)),
        jnp.transpose(down, (1, 2, 0)),
    )


def solution(mesh):
    placed = (
        P("img", "cand", None),
        P("cand"),
        P("cand"),
        P("cand"),
        P(),
        P(),
        P(),
        P("cand", None, None),
        P("cand", None, None),
        P("cand", None, None),
    )
    return jax.shard_map(
        functools.partial(body, mesh.shape["cand"], mesh.shape["img"]),
        mesh=mesh,
        in_specs=placed,
        out_specs=(P("cand", None, "img"), P("cand", None, "img"), P("cand", None, "img")),
        check_vma=False,
    )
```

```python
import functools

import jax
import jax.numpy as jnp
from jax import lax
from jax.experimental import pallas as pl
from jax.experimental.pallas import tpu as pltpu
from jax.sharding import PartitionSpec as P

C = 344
HID = 2064
H = 16
CELLS = 256
CHUNK = 256
FULL = HID // CHUNK
REST = HID - FULL * CHUNK
TILES = 2 * FULL + 1
X = 4
DOWN_ROWS = 384
UP_ROWS = 448
INNER = (6, 7, 8, 11, 12, 13, 16, 17, 18)
F32 = jnp.float32
BF16 = jnp.bfloat16
MESH = pl.DeviceIdType.MESH


def sigmoid(v):
    return 0.5 * jnp.tanh(0.5 * v) + 0.5


def shift_columns(grid, b, col):
    if b == 0:
        return grid
    flat = pltpu.roll(grid.reshape(CELLS, 128), (-b) % CELLS, 0)
    moved = flat.reshape(H, H, 128)
    keep = col < H - b if b > 0 else col >= -b
    return jnp.where(keep, moved, 0.0)


def depthwise(e, tap):
    col = lax.broadcasted_iota(jnp.int32, (H, H, 128), 1)
    grid = e.reshape(H, H, 128)
    zero = jnp.zeros((2, H, 128), F32)
    total = None
    for b in range(-2, 3):
        moved = jnp.concatenate([zero, shift_columns(grid, b, col), zero], 0)
        for a in range(5):
            term = tap(5 * a + b + 2)[None, None, :] * moved[a : a + H]
            total = term if total is None else total + term
    return total.reshape(CELLS, 128)


def depthwise_row(e, tap):
    col = lax.broadcasted_iota(jnp.int32, (5, H, 128), 1)
    total = None
    for b in range(-2, 3):
        if b == 0:
            moved = e.reshape(5, H, 128)
        else:
            moved = pltpu.roll(e, (-b) % (5 * H), 0).reshape(5, H, 128)
            moved = jnp.where(col < H - b if b > 0 else col >= -b, moved, 0.0)
        for a in range(5):
            term = tap(5 * a + b + 2)[None, :] * moved[a]
            total = term if total is None else total + term
    return total


def finish(gu_hbm, gk_hbm, gd_hbm, up_ref, dw_ref, down_ref, gu, gk, gd, sem):
    own = CHUNK + 2
    copies = [
        pltpu.make_async_copy(src, dst, sem.at[k])
        for k, (src, dst) in enumerate(((gu_hbm, gu), (gk_hbm, gk), (gd_hbm, gd)))
    ]
    for copy in copies:
        copy.start()
    copies[0].wait()
    up_ref[:, 0, :] = jnp.transpose(gu[...])[:own, :C]
    copies[1].wait()
    dw_ref[:, 0, :] = gk[:25, :own]
    copies[2].wait()
    down_ref[:, 0, :] = jnp.transpose(gd[...])[:own, :C]


def kernel(
    n_cand,
    n_img,
    x_ref,
    layer_ref,
    expand_ref,
    radius_ref,
    tu_hbm,
    tk_hbm,
    td_hbm,
    cu_hbm,
    ck_hbm,
    cd_hbm,
    gu_ref,
    gk_ref,
    gd_ref,
    tu,
    tk,
    td,
    cu,
    ck,
    cd,
    left_u,
    left_d,
    left_k,
    xg,
    x0,
    xb,
    xt,
    acc,
    acc2,
    eb,
    ebt,
    e_s,
    sp_s,
    sk_s,
    g_s,
    p_s,
    rows,
    kg,
    down_own,
    down_y,
    down_sum,
    down_x,
    up_own,
    up_x,
    up_sum,
    up_y,
    w_sem,
    xs_sem,
    xr_sem,
    down_sem,
    up_sem,
    base,
    xpad,
    xh,
    row_out,
    row_in,
    pair_sem,
    ts_sem,
    tr_sem,
):
    me_c = lax.axis_index("cand")
    me_i = lax.axis_index("img")

    copies = []
    for layer in range(2):
        for src, dst in ((tu_hbm, tu), (td_hbm, td)):
            copies.append(pltpu.make_async_copy(src.at[layer], dst.at[layer], w_sem.at[len(copies)]))
    copies.insert(0, pltpu.make_async_copy(tk_hbm, tk, w_sem.at[len(copies)]))
    for src, dst in ((cu_hbm.at[0], cu), (ck_hbm, ck), (cd_hbm.at[0], cd)):
        copies.append(pltpu.make_async_copy(src, dst, w_sem.at[len(copies)]))
    for copy in copies:
        copy.start()

    xh[...] = x_ref[0].astype(BF16)
    barrier = pltpu.get_barrier_semaphore()

    def greet_cand(k, carry):
        peer = lax.rem(me_c + k, n_cand)
        pl.semaphore_signal(barrier, inc=1, device_id={"cand": peer}, device_id_type=MESH)
        return carry

    def greet_img(k, carry):
        peer = lax.rem(me_i + k, n_img)
        pl.semaphore_signal(barrier, inc=1, device_id={"img": peer}, device_id_type=MESH)
        return carry

    lax.fori_loop(1, n_cand, greet_cand, 0)
    lax.fori_loop(1, n_img, greet_img, 0)
    pl.semaphore_wait(barrier, n_cand + n_img - 2)

    def map_copy(k):
        peer = lax.rem(me_c + k, n_cand)
        return pltpu.make_async_remote_copy(
            src_ref=xh,
            dst_ref=xg.at[me_c],
            send_sem=xs_sem.at[k],
            recv_sem=xr_sem.at[me_c],
            device_id={"cand": peer},
            device_id_type=MESH,
        )

    def map_arrival(k):
        source = lax.rem(me_c + k, n_cand)
        return pltpu.make_async_remote_copy(
            src_ref=xh,
            dst_ref=xg.at[source],
            send_sem=xs_sem.at[k],
            recv_sem=xr_sem.at[source],
            device_id={"cand": source},
            device_id_type=MESH,
        )

    def start_map(k, carry):
        map_copy(k).start()
        return carry

    def wait_map(k, carry):
        map_arrival(k).wait_recv()
        return carry

    def wait_sent(k, carry):
        map_copy(k).wait_send()
        return carry

    lax.fori_loop(1, n_cand, start_map, 0)
    xg[me_c] = xh[...]

    rows[...] = jnp.zeros_like(rows)
    xpad[...] = jnp.zeros_like(xpad)
    kg[...] = jnp.zeros_like(kg)
    left_u[...] = jnp.zeros_like(left_u)
    left_d[...] = jnp.zeros_like(left_d)
    left_k[...] = jnp.zeros_like(left_k)

    layer_here = layer_ref[0]
    units_used = expand_ref[0] * (HID // 2)
    outer = jnp.where(radius_ref[0] >= 2, 1.0, 0.0).astype(F32)

    def tap_mask(shape):
        row = lax.broadcasted_iota(jnp.int32, shape, 0)
        inner = row == INNER[0]
        for other in INNER[1:]:
            inner = inner | (row == other)
        return jnp.where(inner, 1.0, outer)

    def unit_mask(tile):
        unit = lax.broadcasted_iota(jnp.int32, (1, 128), 1) + tile * 128
        return jnp.where(unit < units_used, 1.0, 0.0)

    def border_mask():
        place = lax.broadcasted_iota(jnp.int32, (1, 128), 1)
        unit = ((place >> 4) + 1) * CHUNK + (place & 15)
        return jnp.where(unit < units_used, 1.0, 0.0)

    def lanes(j):
        return pl.ds(pl.multiple_of(j * CHUNK, CHUNK), CHUNK)

    def tile_lanes(tile):
        return pl.ds(pl.multiple_of(tile * 128, 128), 128)

    def active(p, conv):
        k = conv(p * sigmoid(p))
        return (k * sigmoid(k)).astype(BF16)

    def whole_map(tap):
        return lambda e: depthwise(e, tap)

    def one_row(tap):
        return lambda e: depthwise_row(e, tap)

    def load_left(layer):
        left_u[layer, :, :REST] = tu[layer, :, FULL * CHUNK :]
        left_d[layer, :, :REST] = td[layer, :, FULL * CHUNK :]
        left_k[layer, :25, :REST] = tk[:, layer, FULL * CHUNK :]

    core = lax.rem(me_c, 2)
    map_row = me_c // 2

    def teacher_first():
        p = jnp.dot(xb[...], left_u[0], preferred_element_type=F32)
        g = active(p, whole_map(lambda i: left_k[0, i, :]))
        rest = lax.dot_general(g, left_d[0], (((1,), (1,)), ((), ())), preferred_element_type=F32)
        acc[...] = jnp.where(core == 0, rest, 0.0)

        def step(t, carry):
            j = core * (FULL // 2) + t
            p_s[...] = jnp.dot(xb[...], tu[0, :, lanes(j)], preferred_element_type=F32)
            for half in range(2):
                part = slice(128 * half, 128 * half + 128)
                tile = 2 * j + half
                g_s[FULL, :, part] = active(
                    p_s[:, part], whole_map(lambda i: tk[i, 0, tile_lanes(tile)])
                )
            acc[...] += lax.dot_general(
                g_s[FULL], td[0, :, lanes(j)], (((1,), (1,)), ((), ())), preferred_element_type=F32
            )
            return carry

        lax.fori_loop(0, FULL // 2, step, 0)

    def pair_copy():
        return pltpu.make_async_remote_copy(
            src_ref=acc,
            dst_ref=acc2,
            send_sem=pair_sem.at[0],
            recv_sem=pair_sem.at[1],
            device_id={"cand": me_c + 1 - 2 * core},
            device_id_type=MESH,
        )

    def teacher_row():
        near = xpad[pl.ds(pl.multiple_of(map_row * H, H), 5 * H), :]
        p = jnp.dot(near, left_u[1], preferred_element_type=F32)
        g = active(p, one_row(lambda i: left_k[1, i, :]))
        rest = lax.dot_general(g, left_d[1], (((1,), (1,)), ((), ())), preferred_element_type=F32)

        def step(j, total):
            p = jnp.dot(
                xpad[pl.ds(pl.multiple_of(map_row * H, H), 5 * H), :],
                tu[1, :, lanes(j)],
                preferred_element_type=F32,
            )
            parts = []
            for half in range(2):
                tile = 2 * j + half
                parts.append(
                    active(
                        p[:, 128 * half : 128 * half + 128],
                        one_row(lambda i: tk[i, 1, tile_lanes(tile)]),
                    )
                )
            return total + lax.dot_general(
                jnp.concatenate(parts, 1),
                td[1, :, lanes(j)],
                (((1,), (1,)), ((), ())),
                preferred_element_type=F32,
            )

        row_out[...] = lax.fori_loop(0, FULL, step, rest).astype(BF16)

    def row_copy(k):
        peer = lax.rem(me_c + 2 * k, n_cand)
        return pltpu.make_async_remote_copy(
            src_ref=row_out,
            dst_ref=row_in.at[map_row],
            send_sem=ts_sem.at[k],
            recv_sem=tr_sem.at[map_row],
            device_id={"cand": peer},
            device_id_type=MESH,
        )

    def row_arrival(k):
        source = lax.rem(map_row + k, H)
        return pltpu.make_async_remote_copy(
            src_ref=row_out,
            dst_ref=row_in.at[source],
            send_sem=ts_sem.at[k],
            recv_sem=tr_sem.at[source],
            device_id={"cand": lax.rem(me_c + 2 * k, n_cand)},
            device_id_type=MESH,
        )

    def start_row(k, carry):
        row_copy(k).start()
        return carry

    def wait_row(k, carry):
        row_arrival(k).wait_recv()
        return carry

    def sent_row(k, carry):
        row_copy(k).wait_send()
        return carry

    for copy in copies:
        copy.wait()
    load_left(0)
    load_left(1)
    ck[...] = ck[...] * tap_mask((25, 1, HID))
    lane = lax.broadcasted_iota(jnp.int32, (1, 128), 1)

    def borders(block, rows_of):
        whole = jnp.zeros((rows_of, 128), F32)
        for k in range(n_img):
            part = block(k + 1).astype(F32)
            part = part if k == 0 else pltpu.roll(part, REST * k, 1)
            whole = jnp.where((lane >> 4) == k, part, whole)
        return whole

    def wide_tile(ref, k):
        if k == FULL:
            return jnp.concatenate([ref[:, FULL * CHUNK :], jnp.zeros((C, 128 - REST), BF16)], 1)
        return ref[:, k * CHUNK : k * CHUNK + 128]

    def tap_tile(k):
        if k == FULL:
            return jnp.concatenate(
                [ck[:, 0, FULL * CHUNK :], jnp.zeros((25, 128 - REST), F32)], 1
            )
        return ck[:, 0, k * CHUNK : k * CHUNK + 128]

    left_u[2] = borders(lambda k: wide_tile(cu, k), C).astype(BF16)
    edge_down = borders(lambda k: wide_tile(cd, k), C)
    left_d[2] = edge_down.astype(BF16)
    left_d[3] = jnp.where(lane >= 128 - REST, edge_down, 0.0).astype(BF16)
    left_k[2, :25] = borders(tap_tile, 25)

    lax.fori_loop(1, n_cand, wait_map, 0)
    x_wide = xg[...].astype(F32).reshape(CELLS, C)
    x0[...] = x_wide
    xb[...] = x_wide.astype(BF16)
    teacher_first()
    pair = pair_copy()
    pair.start()
    pair.wait()
    ones = x0[...] + (acc[...] + acc2[...])
    base[...] = acc[...] + acc2[...]
    xpad[2 * H : 2 * H + CELLS] = ones.astype(BF16)
    teacher_row()
    first = layer_here == 0
    wide = jnp.where(first, x0[...], ones)
    xb[...] = wide.astype(BF16)
    pad = jnp.zeros((CELLS, 384 - C), F32)
    xt[...] = jnp.transpose(jnp.concatenate([wide, pad], 1))[:C].astype(BF16)

    def forward_tile(p, tile, tap, mask):
        s = sigmoid(p) * mask
        e = p * s
        e_s[tile] = e
        sp_s[tile] = s + e * (1.0 - s)
        k = depthwise(e, tap)
        s2 = sigmoid(k)
        g = k * s2
        sk_s[tile] = s2 + g * (1.0 - s2)
        return g.astype(BF16)

    p = jnp.dot(xb[...], left_u[2], preferred_element_type=F32)
    g = forward_tile(p, 2 * FULL, lambda i: left_k[2, i, :], border_mask())
    g_s[FULL, :, :128] = g
    acc2[...] = lax.dot_general(g, left_d[3], (((1,), (1,)), ((), ())), preferred_element_type=F32)

    lax.fori_loop(1, H, start_row, 0)
    row_in[map_row] = row_out[...]

    def forward(j, carry):
        p_s[...] = jnp.dot(xb[...], cu[:, lanes(j)], preferred_element_type=F32)
        for half in range(2):
            part = slice(128 * half, 128 * half + 128)
            tile = 2 * j + half
            g_s[j, :, part] = forward_tile(
                p_s[:, part], tile, lambda i: ck[i, 0, tile_lanes(tile)], unit_mask(tile)
            )
        acc2[...] += lax.dot_general(
            g_s[j], cd[:, lanes(j)], (((1,), (1,)), ((), ())), preferred_element_type=F32
        )
        return carry

    lax.fori_loop(0, FULL, forward, 0)

    lax.fori_loop(1, H, wait_row, 0)
    second = row_in[...].astype(F32).reshape(CELLS, C)
    error = (acc2[...] - jnp.where(first, base[...], second)) * (1.0 / n_img)
    eb[...] = error.astype(BF16)
    ebt[...] = jnp.transpose(jnp.concatenate([error, pad], 1))[:C].astype(BF16)

    my_x = lax.rem(me_i, X)
    my_y = me_i // X

    def send(src, dst, sems, peer):
        return pltpu.make_async_remote_copy(
            src_ref=src,
            dst_ref=dst,
            send_sem=sems[0],
            recv_sem=sems[1],
            device_id={"img": peer},
            device_id_type=MESH,
        )

    def down_over_y(x):
        slab = X * (1 - my_y) + x
        return send(
            down_own.at[slab],
            down_y.at[x],
            (down_sem.at[0, 0, x], down_sem.at[0, 1, x]),
            X * (1 - my_y) + my_x,
        )

    def down_over_x(x, source):
        return send(
            down_sum.at[x],
            down_x.at[source],
            (down_sem.at[1, 0, x], down_sem.at[1, 1, source]),
            X * my_y + x,
        )

    def up_over_x(y, x, source):
        return send(
            up_own.at[X * y + x],
            up_x.at[y, source],
            (up_sem.at[0, y, x], up_sem.at[1, y, source]),
            X * my_y + x,
        )

    def up_over_y():
        return send(
            up_sum, up_y, (up_sem.at[0, 2, 0], up_sem.at[1, 2, 0]), X * (1 - my_y) + my_x
        )

    def turn(block, other):
        return jnp.dot(
            jnp.transpose(block).astype(BF16), other, preferred_element_type=F32
        ).astype(BF16)

    def place_heads(ref, heads):
        for k in range(n_img):
            part = slice(REST * k, REST * k + REST)
            ref[k, 352:368, :] = heads[part, :CHUNK]
            ref[k, 368:384, : C - CHUNK] = heads[part, CHUNK:]

    place_heads(down_own, turn(g_s[FULL, :, :128].astype(F32), eb[...]))

    def down_slab(y, x):
        j = X * y + x
        down_own[j, :C] = jnp.dot(ebt[...], g_s[j], preferred_element_type=F32).astype(BF16)

    order = (2, 1, 3, 0)

    for k in order:
        x = lax.rem(my_x + k, X)
        down_slab(1 - my_y, x)
        down_over_y(x).start()

    def own_down(x, carry):
        down_slab(my_y, x)
        return carry

    lax.fori_loop(0, X, own_down, 0)

    def relay_down(x):
        down_over_y(x).wait_recv()
        down_sum[x] = (
            down_own[X * my_y + x].astype(F32) + down_y[x].astype(F32)
        ).astype(BF16)

    def relay_and_send(k):
        x = lax.rem(my_x + k, X)
        relay_down(x)
        down_over_x(x, my_x).start()

    def backward_tile(dg, tile, tap):
        col = lax.broadcasted_iota(jnp.int32, (H, H, 128), 1)
        grid = (dg * sk_s[tile]).reshape(H, H, 128)
        for b in range(-2, 3):
            rows[b + 2, 2 : 2 + H] = shift_columns(grid, -b, col)
        total = [None] * H
        for b in range(-2, 3):
            sums = [None] * 5
            for r in range(H):
                e = e_s[tile, H * r : H * r + H, :]
                for a in range(-2, 3):
                    moved = rows[b + 2, 2 - a + r]
                    term = tap(5 * (a + 2) + b + 2)[None, :] * moved
                    total[r] = term if total[r] is None else total[r] + term
                    q = moved * e
                    q = q[:8] + q[8:]
                    sums[a + 2] = q if sums[a + 2] is None else sums[a + 2] + q
            for a in range(5):
                kg[5 * a + b + 2, :] = jnp.sum(sums[a], axis=0)
        de = jnp.concatenate(total, 0)
        return de * sp_s[tile]

    taps = tap_mask((32, 128))

    dg = jnp.dot(eb[...], left_d[2], preferred_element_type=F32)
    dp = backward_tile(dg, 2 * FULL, lambda i: left_k[2, i, :])
    place_heads(up_own, turn(dp, xb[...]))
    edge = kg[...] * taps
    for k in range(n_img):
        moved = edge if k == 0 else pltpu.roll(edge, 128 - REST * k, 1)
        up_own[k, 416:448, :128] = moved.astype(BF16)

    def up_step(t, carry):
        k = X - 1 - (t >> 1)
        x = lax.rem(my_x + k, X)
        y = lax.rem(my_y + 1 + t, 2)
        j = X * y + x
        p_s[...] = jnp.dot(eb[...], cd[:, lanes(j)], preferred_element_type=F32)
        for half in range(2):
            part = slice(128 * half, 128 * half + 128)
            tile = 2 * j + half
            p_s[:, part] = backward_tile(
                p_s[:, part], tile, lambda i: ck[i, 0, tile_lanes(tile)]
            )
            up_own[j, 384:416, part] = (kg[...] * taps).astype(BF16)
        up_own[j, :C] = jnp.dot(
            xt[...], p_s[...].astype(BF16), preferred_element_type=F32
        ).astype(BF16)

        @pl.when(k > 0)
        def _():
            up_over_x(y, x, my_x).start()

        for when, which in ((3, 2), (5, 1), (7, 3)):

            @pl.when(t == when)
            def _():
                relay_and_send(which)

        return carry

    lax.fori_loop(0, n_img, up_step, 0)

    def sum_x(y):
        total = up_own[X * y + my_x].astype(F32)
        for k in range(1, X):
            source = lax.rem(my_x + k, X)
            up_over_x(y, source, source).wait_recv()
            total = total + up_x[y, source].astype(F32)
        return total

    up_sum[...] = sum_x(1 - my_y).astype(BF16)
    up_over_y().start()
    relay_down(my_x)

    amount = lax.rem(384 - 2 * me_i, 384)
    wide_zero = jnp.zeros((128 - REST, 384), F32)
    lane_zero = jnp.zeros((REST, 384 - C), F32)

    def assemble(total, out):
        heads = jnp.concatenate([total[352:368], total[368:384, : C - CHUNK], lane_zero], 1)
        tail = jnp.transpose(jnp.concatenate([heads, wide_zero], 0))[:C]
        out[:C, :] = pltpu.roll(jnp.concatenate([total[:C], tail], 1), amount, 1)
        out[C:, :] = jnp.zeros((384 - C, 384), F32)

    total = down_sum[my_x].astype(F32)
    for k in range(1, X):
        source = lax.rem(my_x + k, X)
        down_over_x(source, source).wait_recv()
        total = total + down_x[source].astype(F32)
    assemble(total, gd_ref)

    total = sum_x(my_y)
    up_over_y().wait_recv()
    total = total + up_y[...].astype(F32)
    assemble(total, gu_ref)
    gk_ref[...] = pltpu.roll(
        jnp.concatenate([total[384:416], total[416:448, :128]], 1), amount, 1
    )

    lax.fori_loop(1, n_cand, wait_sent, 0)
    lax.fori_loop(1, H, sent_row, 0)

    def sent_y(x, carry):
        down_over_y(x).wait_send()
        return carry

    lax.fori_loop(0, X, sent_y, 0)

    def sent_x(k, carry):
        x = lax.rem(my_x + k, X)
        down_over_x(x, my_x).wait_send()
        up_over_x(0, x, my_x).wait_send()
        up_over_x(1, x, my_x).wait_send()
        return carry

    lax.fori_loop(1, X, sent_x, 0)
    up_over_y().wait_send()


def body(n_cand, n_img, first_maps, layer_of, expand_half, radius, *weights):
    teach_up, teach_dw, teach_down, cand_up, cand_dw, cand_down = weights
    vmem = pl.BlockSpec(memory_space=pltpu.VMEM)
    smem = pl.BlockSpec(memory_space=pltpu.SMEM)
    hbm = pl.BlockSpec(memory_space=pl.ANY)
    own = CHUNK + 2
    grads = pl.pallas_call(
        functools.partial(kernel, n_cand, n_img),
        out_shape=(
            jax.ShapeDtypeStruct((384, 384), F32),
            jax.ShapeDtypeStruct((32, 384), F32),
            jax.ShapeDtypeStruct((384, 384), F32),
        ),
        in_specs=[vmem, smem, smem, smem] + [hbm] * 6,
        out_specs=(vmem, vmem, vmem),
        scratch_shapes=[
            pltpu.VMEM((2, C, HID), BF16),
            pltpu.VMEM((25, 2, HID), F32),
            pltpu.VMEM((2, C, HID), BF16),
            pltpu.VMEM((C, HID), BF16),
            pltpu.VMEM((25, 1, HID), F32),
            pltpu.VMEM((C, HID), BF16),
            pltpu.VMEM((3, C, 128), BF16),
            pltpu.VMEM((4, C, 128), BF16),
            pltpu.VMEM((3, 32, 128), F32),
            pltpu.VMEM((n_cand, 8, C), BF16),
            pltpu.VMEM((CELLS, C), F32),
            pltpu.VMEM((CELLS, C), BF16),
            pltpu.VMEM((C, CELLS), BF16),
            pltpu.VMEM((CELLS, C), F32),
            pltpu.VMEM((CELLS, C), F32),
            pltpu.VMEM((CELLS, C), BF16),
            pltpu.VMEM((C, CELLS), BF16),
            pltpu.VMEM((TILES, CELLS, 128), F32),
            pltpu.VMEM((TILES, CELLS, 128), F32),
            pltpu.VMEM((TILES, CELLS, 128), F32),
            pltpu.VMEM((FULL + 1, CELLS, CHUNK), BF16),
            pltpu.VMEM((CELLS, CHUNK), F32),
            pltpu.VMEM((5, H + 4, H, 128), F32),
            pltpu.VMEM((32, 128), F32),
            pltpu.VMEM((n_img, DOWN_ROWS, CHUNK), BF16),
            pltpu.VMEM((X, DOWN_ROWS, CHUNK), BF16),
            pltpu.VMEM((X, DOWN_ROWS, CHUNK), BF16),
            pltpu.VMEM((X, DOWN_ROWS, CHUNK), BF16),
            pltpu.VMEM((n_img, UP_ROWS, CHUNK), BF16),
            pltpu.VMEM((2, X, UP_ROWS, CHUNK), BF16),
            pltpu.VMEM((UP_ROWS, CHUNK), BF16),
            pltpu.VMEM((UP_ROWS, CHUNK), BF16),
            pltpu.SemaphoreType.DMA((9,)),
            pltpu.SemaphoreType.DMA((n_cand,)),
            pltpu.SemaphoreType.DMA((n_cand,)),
            pltpu.SemaphoreType.DMA((2, 2, X)),
            pltpu.SemaphoreType.DMA((2, 3, X)),
            pltpu.VMEM((CELLS, C), F32),
            pltpu.VMEM((CELLS + 4 * H, C), BF16),
            pltpu.VMEM((8, C), BF16),
            pltpu.VMEM((H, C), BF16),
            pltpu.VMEM((H, H, C), BF16),
            pltpu.SemaphoreType.DMA((2,)),
            pltpu.SemaphoreType.DMA((H,)),
            pltpu.SemaphoreType.DMA((H,)),
        ],
        compiler_params=pltpu.CompilerParams(
            collective_id=0, has_side_effects=True, vmem_limit_bytes=56 * 1024 * 1024
        ),
        name="step",
    )(
        first_maps,
        layer_of,
        expand_half,
        radius,
        teach_up,
        jnp.transpose(teach_dw, (1, 0, 2)),
        teach_down,
        cand_up,
        jnp.transpose(cand_dw, (1, 0, 2)),
        cand_down,
    )
    up, dw, down = pl.pallas_call(
        finish,
        out_shape=(
            jax.ShapeDtypeStruct((own, 1, C), F32),
            jax.ShapeDtypeStruct((25, 1, own), F32),
            jax.ShapeDtypeStruct((own, 1, C), F32),
        ),
        in_specs=[hbm] * 3,
        out_specs=(vmem, vmem, vmem),
        scratch_shapes=[
            pltpu.VMEM((384, 384), F32),
            pltpu.VMEM((32, 384), F32),
            pltpu.VMEM((384, 384), F32),
            pltpu.SemaphoreType.DMA((3,)),
        ],
        compiler_params=pltpu.CompilerParams(vmem_limit_bytes=8 * 1024 * 1024),
        name="finish",
    )(*grads)
    return (
        jnp.transpose(up, (1, 2, 0)),
        jnp.transpose(dw, (1, 0, 2)),
        jnp.transpose(down, (1, 2, 0)),
    )


def solution(mesh):
    placed = (
        P("img", "cand", None),
        P("cand"),
        P("cand"),
        P("cand"),
        P(),
        P(),
        P(),
        P("cand", None, None),
        P("cand", None, None),
        P("cand", None, None),
    )
    return jax.shard_map(
        functools.partial(body, mesh.shape["cand"], mesh.shape["img"]),
        mesh=mesh,
        in_specs=placed,
        out_specs=(P("cand", None, "img"), P("cand", None, "img"), P("cand", None, "img")),
        check_vma=False,
    )
```

```python
import functools

import jax
import jax.numpy as jnp
from jax import lax
from jax.experimental import pallas as pl
from jax.experimental.pallas import tpu as pltpu
from jax.sharding import PartitionSpec as P

C = 344
HID = 2064
H = 16
CELLS = 256
CHUNK = 256
FULL = HID // CHUNK
REST = HID - FULL * CHUNK
TILES = 2 * FULL + 1
X = 4
DOWN_ROWS = 384
UP_ROWS = 416
PLACES = 1914
SIDES = 166
HALF = DOWN_ROWS // 2
INNER = (6, 7, 8, 11, 12, 13, 16, 17, 18)
F32 = jnp.float32
BF16 = jnp.bfloat16
MESH = pl.DeviceIdType.MESH


def sigmoid(v):
    return 0.5 * jnp.tanh(0.5 * v) + 0.5


def shift_columns(grid, b, col):
    if b == 0:
        return grid
    flat = pltpu.roll(grid.reshape(CELLS, 128), (-b) % CELLS, 0)
    moved = flat.reshape(H, H, 128)
    keep = col < H - b if b > 0 else col >= -b
    return jnp.where(keep, moved, 0.0)


def depthwise(e, tap):
    col = lax.broadcasted_iota(jnp.int32, (H, H, 128), 1)
    grid = e.reshape(H, H, 128)
    zero = jnp.zeros((2, H, 128), F32)
    total = None
    for b in range(-2, 3):
        moved = jnp.concatenate([zero, shift_columns(grid, b, col), zero], 0)
        for a in range(5):
            term = tap(5 * a + b + 2)[None, None, :] * moved[a : a + H]
            total = term if total is None else total + term
    return total.reshape(CELLS, 128)


def depthwise_row(e, tap):
    col = lax.broadcasted_iota(jnp.int32, (5, H, 128), 1)
    total = None
    for b in range(-2, 3):
        if b == 0:
            moved = e.reshape(5, H, 128)
        else:
            moved = pltpu.roll(e, (-b) % (5 * H), 0).reshape(5, H, 128)
            moved = jnp.where(col < H - b if b > 0 else col >= -b, moved, 0.0)
        for a in range(5):
            term = tap(5 * a + b + 2)[None, :] * moved[a]
            total = term if total is None else total + term
    return total


def finish(gu_hbm, gk_hbm, gd_hbm, up_ref, dw_ref, down_ref, gu, gk, gd, sem):
    own = CHUNK + 2
    copies = [
        pltpu.make_async_copy(src, dst, sem.at[k])
        for k, (src, dst) in enumerate(((gu_hbm, gu), (gk_hbm, gk), (gd_hbm, gd)))
    ]
    for copy in copies:
        copy.start()
    copies[0].wait()
    up_ref[:, 0, :] = jnp.transpose(gu[...])[:own, :C]
    copies[1].wait()
    dw_ref[:, 0, :] = gk[:25, :own]
    copies[2].wait()
    down_ref[:, 0, :] = jnp.transpose(gd[...])[:own, :C]


def kernel(
    n_cand,
    n_img,
    x_ref,
    layer_ref,
    expand_ref,
    radius_ref,
    tu_hbm,
    tk_hbm,
    td_hbm,
    cu_hbm,
    ck_hbm,
    cd_hbm,
    gu_ref,
    gk_ref,
    gd_ref,
    tu,
    tk,
    td,
    cu,
    ck,
    cd,
    left_u,
    left_d,
    left_k,
    xg,
    x0,
    xb,
    xt,
    acc,
    acc2,
    eb,
    ebt,
    e_s,
    sp_s,
    sk_s,
    g_s,
    p_s,
    rows,
    kg,
    down_own,
    down_y,
    down_sum,
    down_x,
    up_own,
    up_x,
    up_sum,
    up_y,
    down_relay,
    up_relay,
    w_sem,
    xs_sem,
    xr_sem,
    down_sem,
    up_sem,
    base,
    xpad,
    xh,
    row_out,
    row_in,
    pair_sem,
    ts_sem,
    tr_sem,
):
    me_c = lax.axis_index("cand")
    me_i = lax.axis_index("img")

    copies = []
    for layer in range(2):
        for src, dst in ((tu_hbm, tu), (td_hbm, td)):
            copies.append(pltpu.make_async_copy(src.at[layer], dst.at[layer], w_sem.at[len(copies)]))
    copies.insert(0, pltpu.make_async_copy(tk_hbm, tk, w_sem.at[len(copies)]))
    for src, dst in ((cu_hbm.at[0], cu), (ck_hbm, ck), (cd_hbm.at[0], cd)):
        copies.append(pltpu.make_async_copy(src, dst, w_sem.at[len(copies)]))
    for copy in copies:
        copy.start()

    xh[...] = x_ref[0].astype(BF16)
    barrier = pltpu.get_barrier_semaphore()

    def greet_cand(k, carry):
        peer = lax.rem(me_c + k, n_cand)
        pl.semaphore_signal(barrier, inc=1, device_id={"cand": peer}, device_id_type=MESH)
        return carry

    def greet_img(k, carry):
        peer = lax.rem(me_i + k, n_img)
        pl.semaphore_signal(barrier, inc=1, device_id={"img": peer}, device_id_type=MESH)
        return carry

    lax.fori_loop(1, n_cand, greet_cand, 0)
    lax.fori_loop(1, n_img, greet_img, 0)
    pl.semaphore_wait(barrier, n_cand + n_img - 2)

    def map_copy(k):
        peer = lax.rem(me_c + k, n_cand)
        return pltpu.make_async_remote_copy(
            src_ref=xh,
            dst_ref=xg.at[me_c],
            send_sem=xs_sem.at[k],
            recv_sem=xr_sem.at[me_c],
            device_id={"cand": peer},
            device_id_type=MESH,
        )

    def map_arrival(k):
        source = lax.rem(me_c + k, n_cand)
        return pltpu.make_async_remote_copy(
            src_ref=xh,
            dst_ref=xg.at[source],
            send_sem=xs_sem.at[k],
            recv_sem=xr_sem.at[source],
            device_id={"cand": source},
            device_id_type=MESH,
        )

    def start_map(k, carry):
        map_copy(k).start()
        return carry

    def wait_map(k, carry):
        map_arrival(k).wait_recv()
        return carry

    def wait_sent(k, carry):
        map_copy(k).wait_send()
        return carry

    lax.fori_loop(1, n_cand, start_map, 0)
    xg[me_c] = xh[...]

    rows[...] = jnp.zeros_like(rows)
    xpad[...] = jnp.zeros_like(xpad)
    kg[...] = jnp.zeros_like(kg)
    left_u[...] = jnp.zeros_like(left_u)
    left_d[...] = jnp.zeros_like(left_d)
    left_k[...] = jnp.zeros_like(left_k)

    layer_here = layer_ref[0]
    units_used = expand_ref[0] * (HID // 2)
    outer = jnp.where(radius_ref[0] >= 2, 1.0, 0.0).astype(F32)

    def tap_mask(shape):
        row = lax.broadcasted_iota(jnp.int32, shape, 0)
        inner = row == INNER[0]
        for other in INNER[1:]:
            inner = inner | (row == other)
        return jnp.where(inner, 1.0, outer)

    def unit_mask(tile):
        unit = lax.broadcasted_iota(jnp.int32, (1, 128), 1) + tile * 128
        return jnp.where(unit < units_used, 1.0, 0.0)

    def border_mask():
        place = lax.broadcasted_iota(jnp.int32, (1, 128), 1)
        unit = ((place >> 4) + 1) * CHUNK + (place & 15)
        return jnp.where(unit < units_used, 1.0, 0.0)

    def lanes(j):
        return pl.ds(pl.multiple_of(j * CHUNK, CHUNK), CHUNK)

    def tile_lanes(tile):
        return pl.ds(pl.multiple_of(tile * 128, 128), 128)

    def active(p, conv):
        k = conv(p * sigmoid(p))
        return (k * sigmoid(k)).astype(BF16)

    def whole_map(tap):
        return lambda e: depthwise(e, tap)

    def one_row(tap):
        return lambda e: depthwise_row(e, tap)

    def load_left(layer):
        left_u[layer, :, :REST] = tu[layer, :, FULL * CHUNK :]
        left_d[layer, :, :REST] = td[layer, :, FULL * CHUNK :]
        left_k[layer, :25, :REST] = tk[:, layer, FULL * CHUNK :]

    core = lax.rem(me_c, 2)
    map_row = me_c // 2

    def teacher_first():
        p = jnp.dot(xb[...], left_u[0], preferred_element_type=F32)
        g = active(p, whole_map(lambda i: left_k[0, i, :]))
        rest = lax.dot_general(g, left_d[0], (((1,), (1,)), ((), ())), preferred_element_type=F32)
        acc[...] = jnp.where(core == 0, rest, 0.0)

        def step(t, carry):
            j = core * (FULL // 2) + t
            p_s[...] = jnp.dot(xb[...], tu[0, :, lanes(j)], preferred_element_type=F32)
            for half in range(2):
                part = slice(128 * half, 128 * half + 128)
                tile = 2 * j + half
                g_s[FULL, :, part] = active(
                    p_s[:, part], whole_map(lambda i: tk[i, 0, tile_lanes(tile)])
                )
            acc[...] += lax.dot_general(
                g_s[FULL], td[0, :, lanes(j)], (((1,), (1,)), ((), ())), preferred_element_type=F32
            )
            return carry

        lax.fori_loop(0, FULL // 2, step, 0)

    def pair_copy():
        return pltpu.make_async_remote_copy(
            src_ref=acc,
            dst_ref=acc2,
            send_sem=pair_sem.at[0],
            recv_sem=pair_sem.at[1],
            device_id={"cand": me_c + 1 - 2 * core},
            device_id_type=MESH,
        )

    def teacher_row():
        near = xpad[pl.ds(pl.multiple_of(map_row * H, H), 5 * H), :]
        p = jnp.dot(near, left_u[1], preferred_element_type=F32)
        g = active(p, one_row(lambda i: left_k[1, i, :]))
        rest = lax.dot_general(g, left_d[1], (((1,), (1,)), ((), ())), preferred_element_type=F32)

        def step(j, total):
            p = jnp.dot(
                xpad[pl.ds(pl.multiple_of(map_row * H, H), 5 * H), :],
                tu[1, :, lanes(j)],
                preferred_element_type=F32,
            )
            parts = []
            for half in range(2):
                tile = 2 * j + half
                parts.append(
                    active(
                        p[:, 128 * half : 128 * half + 128],
                        one_row(lambda i: tk[i, 1, tile_lanes(tile)]),
                    )
                )
            return total + lax.dot_general(
                jnp.concatenate(parts, 1),
                td[1, :, lanes(j)],
                (((1,), (1,)), ((), ())),
                preferred_element_type=F32,
            )

        row_out[...] = lax.fori_loop(0, FULL, step, rest).astype(BF16)

    def row_copy(k):
        peer = lax.rem(me_c + 2 * k, n_cand)
        return pltpu.make_async_remote_copy(
            src_ref=row_out,
            dst_ref=row_in.at[map_row],
            send_sem=ts_sem.at[k],
            recv_sem=tr_sem.at[map_row],
            device_id={"cand": peer},
            device_id_type=MESH,
        )

    def row_arrival(k):
        source = lax.rem(map_row + k, H)
        return pltpu.make_async_remote_copy(
            src_ref=row_out,
            dst_ref=row_in.at[source],
            send_sem=ts_sem.at[k],
            recv_sem=tr_sem.at[source],
            device_id={"cand": lax.rem(me_c + 2 * k, n_cand)},
            device_id_type=MESH,
        )

    def start_row(k, carry):
        row_copy(k).start()
        return carry

    def wait_row(k, carry):
        row_arrival(k).wait_recv()
        return carry

    def sent_row(k, carry):
        row_copy(k).wait_send()
        return carry

    for copy in copies:
        copy.wait()
    load_left(0)
    load_left(1)
    ck[...] = ck[...] * tap_mask((25, 1, HID))
    lane = lax.broadcasted_iota(jnp.int32, (1, 128), 1)

    def borders(block, rows_of):
        whole = jnp.zeros((rows_of, 128), F32)
        for k in range(n_img):
            part = block(k + 1).astype(F32)
            part = part if k == 0 else pltpu.roll(part, REST * k, 1)
            whole = jnp.where((lane >> 4) == k, part, whole)
        return whole

    def wide_tile(ref, k):
        if k == FULL:
            return jnp.concatenate([ref[:, FULL * CHUNK :], jnp.zeros((C, 128 - REST), BF16)], 1)
        return ref[:, k * CHUNK : k * CHUNK + 128]

    def tap_tile(k):
        if k == FULL:
            return jnp.concatenate(
                [ck[:, 0, FULL * CHUNK :], jnp.zeros((25, 128 - REST), F32)], 1
            )
        return ck[:, 0, k * CHUNK : k * CHUNK + 128]

    left_u[2] = borders(lambda k: wide_tile(cu, k), C).astype(BF16)
    edge_down = borders(lambda k: wide_tile(cd, k), C)
    left_d[2] = edge_down.astype(BF16)
    left_d[3] = jnp.where(lane >= 128 - REST, edge_down, 0.0).astype(BF16)
    left_k[2, :25] = borders(tap_tile, 25)

    lax.fori_loop(1, n_cand, wait_map, 0)
    x_wide = xg[...].astype(F32).reshape(CELLS, C)
    x0[...] = x_wide
    xb[...] = x_wide.astype(BF16)
    teacher_first()
    pair = pair_copy()
    pair.start()
    pair.wait()
    ones = x0[...] + (acc[...] + acc2[...])
    base[...] = acc[...] + acc2[...]
    xpad[2 * H : 2 * H + CELLS] = ones.astype(BF16)
    teacher_row()
    first = layer_here == 0
    wide = jnp.where(first, x0[...], ones)
    xb[...] = wide.astype(BF16)
    pad = jnp.zeros((CELLS, 384 - C), F32)
    xt[...] = jnp.transpose(jnp.concatenate([wide, pad], 1))[:C].astype(BF16)

    def forward_tile(p, tile, tap, mask):
        s = sigmoid(p) * mask
        e = p * s
        e_s[tile] = e
        sp_s[tile] = s + e * (1.0 - s)
        k = depthwise(e, tap)
        s2 = sigmoid(k)
        g = k * s2
        sk_s[tile] = s2 + g * (1.0 - s2)
        return g.astype(BF16)

    p = jnp.dot(xb[...], left_u[2], preferred_element_type=F32)
    g = forward_tile(p, 2 * FULL, lambda i: left_k[2, i, :], border_mask())
    g_s[FULL, :, :128] = g
    acc2[...] = lax.dot_general(g, left_d[3], (((1,), (1,)), ((), ())), preferred_element_type=F32)

    lax.fori_loop(1, H, start_row, 0)
    row_in[map_row] = row_out[...]

    def forward(j, carry):
        p_s[...] = jnp.dot(xb[...], cu[:, lanes(j)], preferred_element_type=F32)
        for half in range(2):
            part = slice(128 * half, 128 * half + 128)
            tile = 2 * j + half
            g_s[j, :, part] = forward_tile(
                p_s[:, part], tile, lambda i: ck[i, 0, tile_lanes(tile)], unit_mask(tile)
            )
        acc2[...] += lax.dot_general(
            g_s[j], cd[:, lanes(j)], (((1,), (1,)), ((), ())), preferred_element_type=F32
        )
        return carry

    lax.fori_loop(0, FULL, forward, 0)

    lax.fori_loop(1, H, wait_row, 0)
    second = row_in[...].astype(F32).reshape(CELLS, C)
    error = (acc2[...] - jnp.where(first, base[...], second)) * (1.0 / n_img)
    eb[...] = error.astype(BF16)
    ebt[...] = jnp.transpose(jnp.concatenate([error, pad], 1))[:C].astype(BF16)

    my_x = lax.rem(me_i, X)
    my_y = me_i // X

    def send(src, dst, sems, peer):
        return pltpu.make_async_remote_copy(
            src_ref=src,
            dst_ref=dst,
            send_sem=sems[0],
            recv_sem=sems[1],
            device_id={"img": peer},
            device_id_type=MESH,
        )

    def down_over_y(x):
        slab = X * (1 - my_y) + x
        return send(
            down_own.at[slab],
            down_y.at[x],
            (down_sem.at[0, 0, x], down_sem.at[0, 1, x]),
            X * (1 - my_y) + my_x,
        )

    def down_over_x(x, source):
        return send(
            down_sum.at[x],
            down_x.at[source],
            (down_sem.at[1, 0, x], down_sem.at[1, 1, source]),
            X * my_y + x,
        )

    def up_over_x(y, x, source):
        return send(
            up_own.at[X * y + x],
            up_x.at[y, source],
            (up_sem.at[0, y, x], up_sem.at[1, y, source]),
            X * my_y + x,
        )

    def opposite(h):
        return lax.rem(my_x + 3 - 2 * h, X)

    def down_half(h):
        return send(
            down_sum.at[lax.rem(my_x + 2, X), pl.ds(HALF * h, HALF)],
            down_relay.at[h],
            (down_sem.at[2, 0, h], down_sem.at[2, 1, h]),
            X * my_y + opposite(h),
        )

    def up_half(h):
        return send(
            up_own.at[X * h + lax.rem(my_x + 2, X)],
            up_relay.at[h],
            (up_sem.at[0, 2, 1 + h], up_sem.at[1, 2, 1 + h]),
            X * my_y + opposite(h),
        )

    def up_over_y():
        return send(
            up_sum, up_y, (up_sem.at[0, 2, 0], up_sem.at[1, 2, 0]), X * (1 - my_y) + my_x
        )

    def turn(block, other):
        return jnp.dot(
            jnp.transpose(block).astype(BF16), other, preferred_element_type=F32
        ).astype(BF16)

    def place_heads(ref, heads):
        for k in range(n_img):
            part = slice(REST * k, REST * k + REST)
            ref[k, 352:368, :] = heads[part, :CHUNK]
            ref[k, 368:384, : C - CHUNK] = heads[part, CHUNK:]

    place_heads(down_own, turn(g_s[FULL, :, :128].astype(F32), eb[...]))

    def down_slab(y, x):
        j = X * y + x
        down_own[j, :C] = jnp.dot(ebt[...], g_s[j], preferred_element_type=F32).astype(BF16)

    order = (2, 3, 1, 0)

    for k in order:
        x = lax.rem(my_x + k, X)
        down_slab(1 - my_y, x)
        down_over_y(x).start()

    def own_down(x, carry):
        down_slab(my_y, x)
        return carry

    lax.fori_loop(0, X, own_down, 0)

    def relay_down(x):
        down_over_y(x).wait_recv()
        down_sum[x] = (
            down_own[X * my_y + x].astype(F32) + down_y[x].astype(F32)
        ).astype(BF16)

    def split_down():
        relay_down(lax.rem(my_x + 2, X))
        for h in range(2):
            down_half(h).start()

    def join_down(h):
        x = opposite(h)
        relay_down(x)
        down_half(h).wait_recv()
        part = slice(HALF * h, HALF * h + HALF)
        down_sum[x, part] = (
            down_sum[x, part].astype(F32) + down_relay[h].astype(F32)
        ).astype(BF16)
        down_over_x(x, my_x).start()

    def backward_tile(dg, tile, tap):
        col = lax.broadcasted_iota(jnp.int32, (H, H, 128), 1)
        grid = (dg * sk_s[tile]).reshape(H, H, 128)
        for b in range(-2, 3):
            rows[b + 2, 2 : 2 + H] = shift_columns(grid, -b, col)
        total = [None] * H
        for b in range(-2, 3):
            sums = [None] * 5
            for r in range(H):
                e = e_s[tile, H * r : H * r + H, :]
                for a in range(-2, 3):
                    moved = rows[b + 2, 2 - a + r]
                    term = tap(5 * (a + 2) + b + 2)[None, :] * moved
                    total[r] = term if total[r] is None else total[r] + term
                    q = moved * e
                    q = q[:8] + q[8:]
                    sums[a + 2] = q if sums[a + 2] is None else sums[a + 2] + q
            for a in range(5):
                kg[5 * a + b + 2, :] = jnp.sum(sums[a], axis=0)
        de = jnp.concatenate(total, 0)
        return de * sp_s[tile]

    taps = tap_mask((32, 128))

    dg = jnp.dot(eb[...], left_d[2], preferred_element_type=F32)
    dp = backward_tile(dg, 2 * FULL, lambda i: left_k[2, i, :])
    place_heads(up_own, turn(dp, xb[...]))
    edge = kg[...] * taps
    for k in range(n_img):
        moved = edge if k == 0 else pltpu.roll(edge, 128 - REST * k, 1)
        low = jnp.where(lane < REST, moved[:REST], pltpu.roll(moved[REST:], REST, 1))
        up_own[k, 368:384, 128:] = low.astype(BF16)

    def up_step(t, carry):
        k = (jnp.int32(PLACES) >> (2 * t)) & 3
        x = lax.rem(my_x + k, X)
        y = (jnp.int32(SIDES) >> t) & 1
        j = X * y + x
        p_s[...] = jnp.dot(eb[...], cd[:, lanes(j)], preferred_element_type=F32)
        for half in range(2):
            part = slice(128 * half, 128 * half + 128)
            tile = 2 * j + half
            p_s[:, part] = backward_tile(
                p_s[:, part], tile, lambda i: ck[i, 0, tile_lanes(tile)]
            )
            up_own[j, 384:416, part] = (kg[...] * taps).astype(BF16)
        up_own[j, :C] = jnp.dot(
            xt[...], p_s[...].astype(BF16), preferred_element_type=F32
        ).astype(BF16)

        @pl.when(t < 2)
        def _():
            up_half(t).start()

        @pl.when((t == 4) | (t == 5))
        def _():
            h = t - 4
            up_half(h).wait_recv()
            up_own[j] = (up_own[j].astype(F32) + up_relay[h].astype(F32)).astype(BF16)

        @pl.when((t >= 2) & (t < 6))
        def _():
            up_over_x(y, x, my_x).start()

        @pl.when(t == 3)
        def _():
            split_down()

        @pl.when(t == 7)
        def _():
            join_down(0)

        return carry

    lax.fori_loop(0, n_img, up_step, 0)
    join_down(1)

    def sum_x(y):
        total = up_own[X * y + my_x].astype(F32)
        for k in (1, 3):
            source = lax.rem(my_x + k, X)
            up_over_x(y, source, source).wait_recv()
            total = total + up_x[y, source].astype(F32)
        return total

    up_sum[...] = sum_x(1 - my_y).astype(BF16)
    up_over_y().start()
    relay_down(my_x)

    amount = lax.rem(384 - 2 * me_i, 384)
    wide_zero = jnp.zeros((128 - REST, 384), F32)
    lane_zero = jnp.zeros((REST, 384 - C), F32)

    def assemble(total, out):
        heads = jnp.concatenate([total[352:368], total[368:384, : C - CHUNK], lane_zero], 1)
        tail = jnp.transpose(jnp.concatenate([heads, wide_zero], 0))[:C]
        out[:C, :] = pltpu.roll(jnp.concatenate([total[:C], tail], 1), amount, 1)
        out[C:, :] = jnp.zeros((384 - C, 384), F32)

    total = down_sum[my_x].astype(F32)
    for k in (1, 3):
        source = lax.rem(my_x + k, X)
        down_over_x(source, source).wait_recv()
        total = total + down_x[source].astype(F32)
    assemble(total, gd_ref)

    total = sum_x(my_y)
    up_over_y().wait_recv()
    total = total + up_y[...].astype(F32)
    assemble(total, gu_ref)
    low = total[368:384, 128:]
    edge = jnp.concatenate([low, pltpu.roll(low, 128 - REST, 1)], 0)
    gk_ref[...] = pltpu.roll(
        jnp.concatenate([total[384:416], edge], 1), amount, 1
    )

    lax.fori_loop(1, n_cand, wait_sent, 0)
    lax.fori_loop(1, H, sent_row, 0)

    def sent_y(x, carry):
        down_over_y(x).wait_send()
        return carry

    lax.fori_loop(0, X, sent_y, 0)

    for k in (1, 3):
        x = lax.rem(my_x + k, X)
        down_over_x(x, my_x).wait_send()
        up_over_x(0, x, my_x).wait_send()
        up_over_x(1, x, my_x).wait_send()
    for h in range(2):
        down_half(h).wait_send()
        up_half(h).wait_send()
    up_over_y().wait_send()


def body(n_cand, n_img, first_maps, layer_of, expand_half, radius, *weights):
    teach_up, teach_dw, teach_down, cand_up, cand_dw, cand_down = weights
    vmem = pl.BlockSpec(memory_space=pltpu.VMEM)
    smem = pl.BlockSpec(memory_space=pltpu.SMEM)
    hbm = pl.BlockSpec(memory_space=pl.ANY)
    own = CHUNK + 2
    grads = pl.pallas_call(
        functools.partial(kernel, n_cand, n_img),
        out_shape=(
            jax.ShapeDtypeStruct((384, 384), F32),
            jax.ShapeDtypeStruct((32, 384), F32),
            jax.ShapeDtypeStruct((384, 384), F32),
        ),
        in_specs=[vmem, smem, smem, smem] + [hbm] * 6,
        out_specs=(vmem, vmem, vmem),
        scratch_shapes=[
            pltpu.VMEM((2, C, HID), BF16),
            pltpu.VMEM((25, 2, HID), F32),
            pltpu.VMEM((2, C, HID), BF16),
            pltpu.VMEM((C, HID), BF16),
            pltpu.VMEM((25, 1, HID), F32),
            pltpu.VMEM((C, HID), BF16),
            pltpu.VMEM((3, C, 128), BF16),
            pltpu.VMEM((4, C, 128), BF16),
            pltpu.VMEM((3, 32, 128), F32),
            pltpu.VMEM((n_cand, 8, C), BF16),
            pltpu.VMEM((CELLS, C), F32),
            pltpu.VMEM((CELLS, C), BF16),
            pltpu.VMEM((C, CELLS), BF16),
            pltpu.VMEM((CELLS, C), F32),
            pltpu.VMEM((CELLS, C), F32),
            pltpu.VMEM((CELLS, C), BF16),
            pltpu.VMEM((C, CELLS), BF16),
            pltpu.VMEM((TILES, CELLS, 128), F32),
            pltpu.VMEM((TILES, CELLS, 128), F32),
            pltpu.VMEM((TILES, CELLS, 128), F32),
            pltpu.VMEM((FULL + 1, CELLS, CHUNK), BF16),
            pltpu.VMEM((CELLS, CHUNK), F32),
            pltpu.VMEM((5, H + 4, H, 128), F32),
            pltpu.VMEM((32, 128), F32),
            pltpu.VMEM((n_img, DOWN_ROWS, CHUNK), BF16),
            pltpu.VMEM((X, DOWN_ROWS, CHUNK), BF16),
            pltpu.VMEM((X, DOWN_ROWS, CHUNK), BF16),
            pltpu.VMEM((X, DOWN_ROWS, CHUNK), BF16),
            pltpu.VMEM((n_img, UP_ROWS, CHUNK), BF16),
            pltpu.VMEM((2, X, UP_ROWS, CHUNK), BF16),
            pltpu.VMEM((UP_ROWS, CHUNK), BF16),
            pltpu.VMEM((UP_ROWS, CHUNK), BF16),
            pltpu.VMEM((2, HALF, CHUNK), BF16),
            pltpu.VMEM((2, UP_ROWS, CHUNK), BF16),
            pltpu.SemaphoreType.DMA((9,)),
            pltpu.SemaphoreType.DMA((n_cand,)),
            pltpu.SemaphoreType.DMA((n_cand,)),
            pltpu.SemaphoreType.DMA((3, 2, X)),
            pltpu.SemaphoreType.DMA((2, 3, X)),
            pltpu.VMEM((CELLS, C), F32),
            pltpu.VMEM((CELLS + 4 * H, C), BF16),
            pltpu.VMEM((8, C), BF16),
            pltpu.VMEM((H, C), BF16),
            pltpu.VMEM((H, H, C), BF16),
            pltpu.SemaphoreType.DMA((2,)),
            pltpu.SemaphoreType.DMA((H,)),
            pltpu.SemaphoreType.DMA((H,)),
        ],
        compiler_params=pltpu.CompilerParams(
            collective_id=0, has_side_effects=True, vmem_limit_bytes=56 * 1024 * 1024
        ),
        name="step",
    )(
        first_maps,
        layer_of,
        expand_half,
        radius,
        teach_up,
        jnp.transpose(teach_dw, (1, 0, 2)),
        teach_down,
        cand_up,
        jnp.transpose(cand_dw, (1, 0, 2)),
        cand_down,
    )
    up, dw, down = pl.pallas_call(
        finish,
        out_shape=(
            jax.ShapeDtypeStruct((own, 1, C), F32),
            jax.ShapeDtypeStruct((25, 1, own), F32),
            jax.ShapeDtypeStruct((own, 1, C), F32),
        ),
        in_specs=[hbm] * 3,
        out_specs=(vmem, vmem, vmem),
        scratch_shapes=[
            pltpu.VMEM((384, 384), F32),
            pltpu.VMEM((32, 384), F32),
            pltpu.VMEM((384, 384), F32),
            pltpu.SemaphoreType.DMA((3,)),
        ],
        compiler_params=pltpu.CompilerParams(vmem_limit_bytes=60 * 1024 * 1024),
        name="finish",
    )(*grads)
    return (
        jnp.transpose(up, (1, 2, 0)),
        jnp.transpose(dw, (1, 0, 2)),
        jnp.transpose(down, (1, 2, 0)),
    )


def solution(mesh):
    placed = (
        P("img", "cand", None),
        P("cand"),
        P("cand"),
        P("cand"),
        P(),
        P(),
        P(),
        P("cand", None, None),
        P("cand", None, None),
        P("cand", None, None),
    )
    return jax.shard_map(
        functools.partial(body, mesh.shape["cand"], mesh.shape["img"]),
        mesh=mesh,
        in_specs=placed,
        out_specs=(P("cand", None, "img"), P("cand", None, "img"), P("cand", None, "img")),
        check_vma=False,
    )
```

```python
import functools

import jax
import jax.numpy as jnp
from jax import lax
from jax.experimental import pallas as pl
from jax.experimental.pallas import tpu as pltpu
from jax.sharding import PartitionSpec as P

C = 344
HID = 2064
H = 16
CELLS = 256
CHUNK = 256
FULL = HID // CHUNK
REST = HID - FULL * CHUNK
TILES = 2 * FULL + 1
X = 4
DOWN_ROWS = 384
UP_ROWS = 416
PLACES = 1914
ROW_STEP = 4
SIDES = 166
HALF = DOWN_ROWS // 2
INNER = (6, 7, 8, 11, 12, 13, 16, 17, 18)
F32 = jnp.float32
BF16 = jnp.bfloat16
MESH = pl.DeviceIdType.MESH


def sigmoid(v):
    return 0.5 * jnp.tanh(0.5 * v) + 0.5


def shift_columns(grid, b, col):
    if b == 0:
        return grid
    flat = pltpu.roll(grid.reshape(CELLS, 128), (-b) % CELLS, 0)
    moved = flat.reshape(H, H, 128)
    keep = col < H - b if b > 0 else col >= -b
    return jnp.where(keep, moved, 0.0)


def depthwise(e, tap):
    col = lax.broadcasted_iota(jnp.int32, (H, H, 128), 1)
    grid = e.reshape(H, H, 128)
    zero = jnp.zeros((2, H, 128), F32)
    total = None
    for b in range(-2, 3):
        moved = jnp.concatenate([zero, shift_columns(grid, b, col), zero], 0)
        for a in range(5):
            term = tap(5 * a + b + 2)[None, None, :] * moved[a : a + H]
            total = term if total is None else total + term
    return total.reshape(CELLS, 128)


def depthwise_row(e, tap):
    col = lax.broadcasted_iota(jnp.int32, (5, H, 128), 1)
    total = None
    for b in range(-2, 3):
        if b == 0:
            moved = e.reshape(5, H, 128)
        else:
            moved = pltpu.roll(e, (-b) % (5 * H), 0).reshape(5, H, 128)
            moved = jnp.where(col < H - b if b > 0 else col >= -b, moved, 0.0)
        for a in range(5):
            term = tap(5 * a + b + 2)[None, :] * moved[a]
            total = term if total is None else total + term
    return total


def finish(gu_hbm, gk_hbm, gd_hbm, up_ref, dw_ref, down_ref, gu, gk, gd, sem):
    own = CHUNK + 2
    copies = [
        pltpu.make_async_copy(src, dst, sem.at[k])
        for k, (src, dst) in enumerate(((gu_hbm, gu), (gk_hbm, gk), (gd_hbm, gd)))
    ]
    for copy in copies:
        copy.start()
    copies[0].wait()
    up_ref[:, 0, :] = jnp.transpose(gu[...])[:own, :C]
    copies[1].wait()
    dw_ref[:, 0, :] = gk[:25, :own]
    copies[2].wait()
    down_ref[:, 0, :] = jnp.transpose(gd[...])[:own, :C]


def kernel(
    n_cand,
    n_img,
    x_ref,
    layer_ref,
    expand_ref,
    radius_ref,
    tu_hbm,
    tk_hbm,
    td_hbm,
    cu_hbm,
    ck_hbm,
    cd_hbm,
    gu_ref,
    gk_ref,
    gd_ref,
    tu,
    tk,
    td,
    cu,
    ck,
    cd,
    left_u,
    left_d,
    left_k,
    xg,
    x0,
    xb,
    xt,
    acc,
    acc2,
    eb,
    ebt,
    e_s,
    sp_s,
    sk_s,
    g_s,
    p_s,
    rows,
    kg,
    down_own,
    down_y,
    down_sum,
    down_x,
    up_own,
    up_x,
    up_sum,
    up_y,
    down_relay,
    up_relay,
    g_t,
    w_sem,
    xs_sem,
    xr_sem,
    down_sem,
    up_sem,
    base,
    xpad,
    xh,
    row_out,
    row_in,
    pair_sem,
    ts_sem,
    tr_sem,
):
    me_c = lax.axis_index("cand")
    me_i = lax.axis_index("img")

    copies = []
    for layer in range(2):
        for src, dst in ((tu_hbm, tu), (td_hbm, td)):
            copies.append(pltpu.make_async_copy(src.at[layer], dst.at[layer], w_sem.at[len(copies)]))
    copies.insert(0, pltpu.make_async_copy(tk_hbm, tk, w_sem.at[len(copies)]))
    for src, dst in ((cu_hbm.at[0], cu), (ck_hbm, ck), (cd_hbm.at[0], cd)):
        copies.append(pltpu.make_async_copy(src, dst, w_sem.at[len(copies)]))
    for copy in copies:
        copy.start()

    xh[...] = x_ref[0].astype(BF16)
    barrier = pltpu.get_barrier_semaphore()

    def greet_cand(k, carry):
        peer = lax.rem(me_c + k, n_cand)
        pl.semaphore_signal(barrier, inc=1, device_id={"cand": peer}, device_id_type=MESH)
        return carry

    def greet_img(k, carry):
        peer = lax.rem(me_i + k, n_img)
        pl.semaphore_signal(barrier, inc=1, device_id={"img": peer}, device_id_type=MESH)
        return carry

    lax.fori_loop(1, n_cand, greet_cand, 0)
    lax.fori_loop(1, n_img, greet_img, 0)
    pl.semaphore_wait(barrier, n_cand + n_img - 2)

    def map_copy(k):
        peer = lax.rem(me_c + k, n_cand)
        return pltpu.make_async_remote_copy(
            src_ref=xh,
            dst_ref=xg.at[me_c],
            send_sem=xs_sem.at[k],
            recv_sem=xr_sem.at[me_c],
            device_id={"cand": peer},
            device_id_type=MESH,
        )

    def map_arrival(k):
        source = lax.rem(me_c + k, n_cand)
        return pltpu.make_async_remote_copy(
            src_ref=xh,
            dst_ref=xg.at[source],
            send_sem=xs_sem.at[k],
            recv_sem=xr_sem.at[source],
            device_id={"cand": source},
            device_id_type=MESH,
        )

    def start_map(k, carry):
        map_copy(k).start()
        return carry

    def wait_map(k, carry):
        map_arrival(k).wait_recv()
        return carry

    def wait_sent(k, carry):
        map_copy(k).wait_send()
        return carry

    lax.fori_loop(1, n_cand, start_map, 0)
    xg[me_c] = xh[...]

    rows[...] = jnp.zeros_like(rows)
    xpad[...] = jnp.zeros_like(xpad)
    kg[...] = jnp.zeros_like(kg)
    left_u[...] = jnp.zeros_like(left_u)
    left_d[...] = jnp.zeros_like(left_d)
    left_k[...] = jnp.zeros_like(left_k)

    layer_here = layer_ref[0]
    units_used = expand_ref[0] * (HID // 2)
    outer = jnp.where(radius_ref[0] >= 2, 1.0, 0.0).astype(F32)

    def tap_mask(shape):
        row = lax.broadcasted_iota(jnp.int32, shape, 0)
        inner = row == INNER[0]
        for other in INNER[1:]:
            inner = inner | (row == other)
        return jnp.where(inner, 1.0, outer)

    def unit_mask(tile):
        unit = lax.broadcasted_iota(jnp.int32, (1, 128), 1) + tile * 128
        return jnp.where(unit < units_used, 1.0, 0.0)

    def border_mask():
        place = lax.broadcasted_iota(jnp.int32, (1, 128), 1)
        unit = ((place >> 4) + 1) * CHUNK + (place & 15)
        return jnp.where(unit < units_used, 1.0, 0.0)

    def lanes(j):
        return pl.ds(pl.multiple_of(j * CHUNK, CHUNK), CHUNK)

    def tile_lanes(tile):
        return pl.ds(pl.multiple_of(tile * 128, 128), 128)

    def active(p, conv):
        k = conv(p * sigmoid(p))
        return (k * sigmoid(k)).astype(BF16)

    def whole_map(tap):
        return lambda e: depthwise(e, tap)

    def one_row(tap):
        return lambda e: depthwise_row(e, tap)

    def load_left(layer):
        left_u[layer, :, :REST] = tu[layer, :, FULL * CHUNK :]
        left_d[layer, :, :REST] = td[layer, :, FULL * CHUNK :]
        left_k[layer, :25, :REST] = tk[:, layer, FULL * CHUNK :]

    core = lax.rem(me_c, 2)
    map_row = me_c // 2

    def teacher_first():
        p = jnp.dot(xb[...], left_u[0], preferred_element_type=F32)
        g = active(p, whole_map(lambda i: left_k[0, i, :]))
        rest = lax.dot_general(g, left_d[0], (((1,), (1,)), ((), ())), preferred_element_type=F32)
        acc[...] = jnp.where(core == 0, rest, 0.0)

        def step(t, carry):
            j = core * (FULL // 2) + t
            p_s[0] = jnp.dot(xb[...], tu[0, :, lanes(j)], preferred_element_type=F32)
            for half in range(2):
                part = slice(128 * half, 128 * half + 128)
                tile = 2 * j + half
                g_s[FULL, :, part] = active(
                    p_s[0, :, part], whole_map(lambda i: tk[i, 0, tile_lanes(tile)])
                )
            acc[...] += lax.dot_general(
                g_s[FULL], td[0, :, lanes(j)], (((1,), (1,)), ((), ())), preferred_element_type=F32
            )
            return carry

        lax.fori_loop(0, FULL // 2, step, 0)

    def pair_copy():
        return pltpu.make_async_remote_copy(
            src_ref=acc,
            dst_ref=acc2,
            send_sem=pair_sem.at[0],
            recv_sem=pair_sem.at[1],
            device_id={"cand": me_c + 1 - 2 * core},
            device_id_type=MESH,
        )

    def teacher_row():
        near = xpad[pl.ds(pl.multiple_of(map_row * H, H), 5 * H), :]
        p = jnp.dot(near, left_u[1], preferred_element_type=F32)
        g = active(p, one_row(lambda i: left_k[1, i, :]))
        rest = lax.dot_general(g, left_d[1], (((1,), (1,)), ((), ())), preferred_element_type=F32)

        def step(m, total):
            for k in range(ROW_STEP):
                j = ROW_STEP * m + k
                p = jnp.dot(near, tu[1, :, lanes(j)], preferred_element_type=F32)
                parts = []
                for half in range(2):
                    tile = 2 * j + half
                    parts.append(
                        active(
                            p[:, 128 * half : 128 * half + 128],
                            one_row(lambda i, tile=tile: tk[i, 1, tile_lanes(tile)]),
                        )
                    )
                total = total + lax.dot_general(
                    jnp.concatenate(parts, 1),
                    td[1, :, lanes(j)],
                    (((1,), (1,)), ((), ())),
                    preferred_element_type=F32,
                )
            return total

        row_out[...] = lax.fori_loop(0, FULL // ROW_STEP, step, rest).astype(BF16)

    def row_copy(k):
        peer = lax.rem(me_c + 2 * k, n_cand)
        return pltpu.make_async_remote_copy(
            src_ref=row_out,
            dst_ref=row_in.at[map_row],
            send_sem=ts_sem.at[k],
            recv_sem=tr_sem.at[map_row],
            device_id={"cand": peer},
            device_id_type=MESH,
        )

    def row_arrival(k):
        source = lax.rem(map_row + k, H)
        return pltpu.make_async_remote_copy(
            src_ref=row_out,
            dst_ref=row_in.at[source],
            send_sem=ts_sem.at[k],
            recv_sem=tr_sem.at[source],
            device_id={"cand": lax.rem(me_c + 2 * k, n_cand)},
            device_id_type=MESH,
        )

    def start_row(k, carry):
        row_copy(k).start()
        return carry

    def wait_row(k, carry):
        row_arrival(k).wait_recv()
        return carry

    def sent_row(k, carry):
        row_copy(k).wait_send()
        return carry

    for copy in copies:
        copy.wait()
    load_left(0)
    load_left(1)
    ck[...] = ck[...] * tap_mask((25, 1, HID))
    lane = lax.broadcasted_iota(jnp.int32, (1, 128), 1)

    def borders(block, rows_of):
        whole = jnp.zeros((rows_of, 128), F32)
        for k in range(n_img):
            part = block(k + 1).astype(F32)
            part = part if k == 0 else pltpu.roll(part, REST * k, 1)
            whole = jnp.where((lane >> 4) == k, part, whole)
        return whole

    def wide_tile(ref, k):
        if k == FULL:
            return jnp.concatenate([ref[:, FULL * CHUNK :], jnp.zeros((C, 128 - REST), BF16)], 1)
        return ref[:, k * CHUNK : k * CHUNK + 128]

    def tap_tile(k):
        if k == FULL:
            return jnp.concatenate(
                [ck[:, 0, FULL * CHUNK :], jnp.zeros((25, 128 - REST), F32)], 1
            )
        return ck[:, 0, k * CHUNK : k * CHUNK + 128]

    left_u[2] = borders(lambda k: wide_tile(cu, k), C).astype(BF16)
    edge_down = borders(lambda k: wide_tile(cd, k), C)
    left_d[2] = edge_down.astype(BF16)
    left_d[3] = jnp.where(lane >= 128 - REST, edge_down, 0.0).astype(BF16)
    left_k[2, :25] = borders(tap_tile, 25)

    lax.fori_loop(1, n_cand, wait_map, 0)
    x_wide = xg[...].astype(F32).reshape(CELLS, C)
    x0[...] = x_wide
    xb[...] = x_wide.astype(BF16)
    teacher_first()
    pair = pair_copy()
    pair.start()
    pair.wait()
    ones = x0[...] + (acc[...] + acc2[...])
    base[...] = acc[...] + acc2[...]
    xpad[2 * H : 2 * H + CELLS] = ones.astype(BF16)
    teacher_row()
    lax.fori_loop(1, H, start_row, 0)
    row_in[map_row] = row_out[...]
    first = layer_here == 0
    wide = jnp.where(first, x0[...], ones)
    xb[...] = wide.astype(BF16)
    pad = jnp.zeros((CELLS, 384 - C), F32)
    xt[...] = jnp.transpose(jnp.concatenate([wide, pad], 1))[:C].astype(BF16)

    def forward_tile(p, tile, tap, mask):
        s = sigmoid(p) * mask
        e = p * s
        e_s[tile] = e
        sp_s[tile] = s + e * (1.0 - s)
        k = depthwise(e, tap)
        s2 = sigmoid(k)
        g = k * s2
        sk_s[tile] = s2 + g * (1.0 - s2)
        return g.astype(BF16)

    p = jnp.dot(xb[...], left_u[2], preferred_element_type=F32)
    g = forward_tile(p, 2 * FULL, lambda i: left_k[2, i, :], border_mask())
    g_s[FULL, :, :128] = g
    acc2[...] = lax.dot_general(g, left_d[3], (((1,), (1,)), ((), ())), preferred_element_type=F32)

    def up_product(j, slot):
        p_s[slot] = jnp.dot(xb[...], cu[:, lanes(j)], preferred_element_type=F32)

    def forward(m, carry):
        for slot in range(2):
            j = 2 * m + slot
            up_product(lax.rem(j + 1, FULL), 1 - slot)
            for half in range(2):
                part = slice(128 * half, 128 * half + 128)
                tile = 2 * j + half
                g = forward_tile(
                    p_s[slot, :, part],
                    tile,
                    lambda i, tile=tile: ck[i, 0, tile_lanes(tile)],
                    unit_mask(tile),
                )
                g_t[slot, :, part] = g
                g_s[j, :, part] = g
            acc2[...] += lax.dot_general(
                g_t[slot], cd[:, lanes(j)], (((1,), (1,)), ((), ())), preferred_element_type=F32
            )
        return carry

    up_product(0, 0)
    lax.fori_loop(0, FULL // 2, forward, 0)

    lax.fori_loop(1, H, wait_row, 0)
    second = row_in[...].astype(F32).reshape(CELLS, C)
    error = (acc2[...] - jnp.where(first, base[...], second)) * (1.0 / n_img)
    eb[...] = error.astype(BF16)
    ebt[...] = jnp.transpose(jnp.concatenate([error, pad], 1))[:C].astype(BF16)

    my_x = lax.rem(me_i, X)
    my_y = me_i // X

    def send(src, dst, sems, peer):
        return pltpu.make_async_remote_copy(
            src_ref=src,
            dst_ref=dst,
            send_sem=sems[0],
            recv_sem=sems[1],
            device_id={"img": peer},
            device_id_type=MESH,
        )

    def down_over_y(x):
        slab = X * (1 - my_y) + x
        return send(
            down_own.at[slab],
            down_y.at[x],
            (down_sem.at[0, 0, x], down_sem.at[0, 1, x]),
            X * (1 - my_y) + my_x,
        )

    def down_over_x(x, source):
        return send(
            down_sum.at[x],
            down_x.at[source],
            (down_sem.at[1, 0, x], down_sem.at[1, 1, source]),
            X * my_y + x,
        )

    def up_over_x(y, x, source):
        return send(
            up_own.at[X * y + x],
            up_x.at[y, source],
            (up_sem.at[0, y, x], up_sem.at[1, y, source]),
            X * my_y + x,
        )

    def opposite(h):
        return lax.rem(my_x + 3 - 2 * h, X)

    def down_half(h):
        return send(
            down_sum.at[lax.rem(my_x + 2, X), pl.ds(HALF * h, HALF)],
            down_relay.at[h],
            (down_sem.at[2, 0, h], down_sem.at[2, 1, h]),
            X * my_y + opposite(h),
        )

    def up_half(h):
        return send(
            up_own.at[X * h + lax.rem(my_x + 2, X)],
            up_relay.at[h],
            (up_sem.at[0, 2, 1 + h], up_sem.at[1, 2, 1 + h]),
            X * my_y + opposite(h),
        )

    def up_over_y():
        return send(
            up_sum, up_y, (up_sem.at[0, 2, 0], up_sem.at[1, 2, 0]), X * (1 - my_y) + my_x
        )

    def turn(block, other):
        return jnp.dot(
            jnp.transpose(block).astype(BF16), other, preferred_element_type=F32
        ).astype(BF16)

    def place_heads(ref, heads):
        for k in range(n_img):
            part = slice(REST * k, REST * k + REST)
            ref[k, 352:368, :] = heads[part, :CHUNK]
            ref[k, 368:384, : C - CHUNK] = heads[part, CHUNK:]

    place_heads(down_own, turn(g_s[FULL, :, :128].astype(F32), eb[...]))

    def down_slab(y, x):
        j = X * y + x
        down_own[j, :C] = jnp.dot(ebt[...], g_s[j], preferred_element_type=F32).astype(BF16)

    def start_down(k):
        x = lax.rem(my_x + k, X)
        down_slab(1 - my_y, x)
        down_over_y(x).start()

    start_down(2)

    def relay_down(x):
        j = X * my_y + x
        down_over_y(x).wait_recv()
        own = jnp.dot(ebt[...], g_s[j], preferred_element_type=F32)
        down_sum[x, :C] = (own + down_y[x, :C].astype(F32)).astype(BF16)
        down_sum[x, 352:] = (
            down_own[j, 352:].astype(F32) + down_y[x, 352:].astype(F32)
        ).astype(BF16)

    def split_down():
        relay_down(lax.rem(my_x + 2, X))
        for h in range(2):
            down_half(h).start()

    def join_down(h):
        x = opposite(h)
        relay_down(x)
        down_half(h).wait_recv()
        part = slice(HALF * h, HALF * h + HALF)
        down_sum[x, part] = (
            down_sum[x, part].astype(F32) + down_relay[h].astype(F32)
        ).astype(BF16)
        down_over_x(x, my_x).start()

    def backward_tile(dg, tile, tap):
        col = lax.broadcasted_iota(jnp.int32, (H, H, 128), 1)
        grid = (dg * sk_s[tile]).reshape(H, H, 128)
        for b in range(-2, 3):
            rows[b + 2, 2 : 2 + H] = shift_columns(grid, -b, col)
        total = [None] * H
        for b in range(-2, 3):
            sums = [None] * 5
            for r in range(H):
                e = e_s[tile, H * r : H * r + H, :]
                for a in range(-2, 3):
                    moved = rows[b + 2, 2 - a + r]
                    term = tap(5 * (a + 2) + b + 2)[None, :] * moved
                    total[r] = term if total[r] is None else total[r] + term
                    q = moved * e
                    q = q[:8] + q[8:]
                    sums[a + 2] = q if sums[a + 2] is None else sums[a + 2] + q
            for a in range(5):
                kg[5 * a + b + 2, :] = jnp.sum(sums[a], axis=0)
        de = jnp.concatenate(total, 0)
        return de * sp_s[tile]

    taps = tap_mask((32, 128))

    dg = jnp.dot(eb[...], left_d[2], preferred_element_type=F32)
    dp = backward_tile(dg, 2 * FULL, lambda i: left_k[2, i, :])
    place_heads(up_own, turn(dp, xb[...]))
    edge = kg[...] * taps
    for k in range(n_img):
        moved = edge if k == 0 else pltpu.roll(edge, 128 - REST * k, 1)
        low = jnp.where(lane < REST, moved[:REST], pltpu.roll(moved[REST:], REST, 1))
        up_own[k, 368:384, 128:] = low.astype(BF16)

    def up_step(t, carry):
        k = (jnp.int32(PLACES) >> (2 * t)) & 3
        x = lax.rem(my_x + k, X)
        y = (jnp.int32(SIDES) >> t) & 1
        j = X * y + x
        p_s[0] = jnp.dot(eb[...], cd[:, lanes(j)], preferred_element_type=F32)
        for half in range(2):
            part = slice(128 * half, 128 * half + 128)
            tile = 2 * j + half
            p_s[0, :, part] = backward_tile(
                p_s[0, :, part], tile, lambda i: ck[i, 0, tile_lanes(tile)]
            )
            up_own[j, 384:416, part] = (kg[...] * taps).astype(BF16)
        up_own[j, :C] = jnp.dot(
            xt[...], p_s[0].astype(BF16), preferred_element_type=F32
        ).astype(BF16)

        @pl.when(t < 2)
        def _():
            up_half(t).start()

        for when, which in ((0, 3), (1, 1), (2, 0)):

            @pl.when(t == when)
            def _():
                start_down(which)

        @pl.when((t == 4) | (t == 5))
        def _():
            h = t - 4
            up_half(h).wait_recv()
            up_own[j] = (up_own[j].astype(F32) + up_relay[h].astype(F32)).astype(BF16)

        @pl.when((t >= 2) & (t < 6))
        def _():
            up_over_x(y, x, my_x).start()

        @pl.when(t == 3)
        def _():
            split_down()

        @pl.when(t == 7)
        def _():
            join_down(0)

        return carry

    lax.fori_loop(0, n_img, up_step, 0)
    join_down(1)

    def sum_x(y):
        total = up_own[X * y + my_x].astype(F32)
        for k in (1, 3):
            source = lax.rem(my_x + k, X)
            up_over_x(y, source, source).wait_recv()
            total = total + up_x[y, source].astype(F32)
        return total

    up_sum[...] = sum_x(1 - my_y).astype(BF16)
    up_over_y().start()
    relay_down(my_x)

    amount = lax.rem(384 - 2 * me_i, 384)
    wide_zero = jnp.zeros((128 - REST, 384), F32)
    lane_zero = jnp.zeros((REST, 384 - C), F32)

    def assemble(total, out):
        heads = jnp.concatenate([total[352:368], total[368:384, : C - CHUNK], lane_zero], 1)
        tail = jnp.transpose(jnp.concatenate([heads, wide_zero], 0))[:C]
        out[:C, :] = pltpu.roll(jnp.concatenate([total[:C], tail], 1), amount, 1)
        out[C:, :] = jnp.zeros((384 - C, 384), F32)

    total = down_sum[my_x].astype(F32)
    for k in (1, 3):
        source = lax.rem(my_x + k, X)
        down_over_x(source, source).wait_recv()
        total = total + down_x[source].astype(F32)
    assemble(total, gd_ref)

    total = sum_x(my_y)
    up_over_y().wait_recv()
    total = total + up_y[...].astype(F32)
    assemble(total, gu_ref)
    low = total[368:384, 128:]
    edge = jnp.concatenate([low, pltpu.roll(low, 128 - REST, 1)], 0)
    gk_ref[...] = pltpu.roll(
        jnp.concatenate([total[384:416], edge], 1), amount, 1
    )

    lax.fori_loop(1, n_cand, wait_sent, 0)
    lax.fori_loop(1, H, sent_row, 0)

    def sent_y(x, carry):
        down_over_y(x).wait_send()
        return carry

    lax.fori_loop(0, X, sent_y, 0)

    for k in (1, 3):
        x = lax.rem(my_x + k, X)
        down_over_x(x, my_x).wait_send()
        up_over_x(0, x, my_x).wait_send()
        up_over_x(1, x, my_x).wait_send()
    for h in range(2):
        down_half(h).wait_send()
        up_half(h).wait_send()
    up_over_y().wait_send()


def body(n_cand, n_img, first_maps, layer_of, expand_half, radius, *weights):
    teach_up, teach_dw, teach_down, cand_up, cand_dw, cand_down = weights
    vmem = pl.BlockSpec(memory_space=pltpu.VMEM)
    smem = pl.BlockSpec(memory_space=pltpu.SMEM)
    hbm = pl.BlockSpec(memory_space=pl.ANY)
    own = CHUNK + 2
    grads = pl.pallas_call(
        functools.partial(kernel, n_cand, n_img),
        out_shape=(
            jax.ShapeDtypeStruct((384, 384), F32),
            jax.ShapeDtypeStruct((32, 384), F32),
            jax.ShapeDtypeStruct((384, 384), F32),
        ),
        in_specs=[vmem, smem, smem, smem] + [hbm] * 6,
        out_specs=(vmem, vmem, vmem),
        scratch_shapes=[
            pltpu.VMEM((2, C, HID), BF16),
            pltpu.VMEM((25, 2, HID), F32),
            pltpu.VMEM((2, C, HID), BF16),
            pltpu.VMEM((C, HID), BF16),
            pltpu.VMEM((25, 1, HID), F32),
            pltpu.VMEM((C, HID), BF16),
            pltpu.VMEM((3, C, 128), BF16),
            pltpu.VMEM((4, C, 128), BF16),
            pltpu.VMEM((3, 32, 128), F32),
            pltpu.VMEM((n_cand, 8, C), BF16),
            pltpu.VMEM((CELLS, C), F32),
            pltpu.VMEM((CELLS, C), BF16),
            pltpu.VMEM((C, CELLS), BF16),
            pltpu.VMEM((CELLS, C), F32),
            pltpu.VMEM((CELLS, C), F32),
            pltpu.VMEM((CELLS, C), BF16),
            pltpu.VMEM((C, CELLS), BF16),
            pltpu.VMEM((TILES, CELLS, 128), F32),
            pltpu.VMEM((TILES, CELLS, 128), F32),
            pltpu.VMEM((TILES, CELLS, 128), F32),
            pltpu.VMEM((FULL + 1, CELLS, CHUNK), BF16),
            pltpu.VMEM((2, CELLS, CHUNK), F32),
            pltpu.VMEM((5, H + 4, H, 128), F32),
            pltpu.VMEM((32, 128), F32),
            pltpu.VMEM((n_img, DOWN_ROWS, CHUNK), BF16),
            pltpu.VMEM((X, DOWN_ROWS, CHUNK), BF16),
            pltpu.VMEM((X, DOWN_ROWS, CHUNK), BF16),
            pltpu.VMEM((X, DOWN_ROWS, CHUNK), BF16),
            pltpu.VMEM((n_img, UP_ROWS, CHUNK), BF16),
            pltpu.VMEM((2, X, UP_ROWS, CHUNK), BF16),
            pltpu.VMEM((UP_ROWS, CHUNK), BF16),
            pltpu.VMEM((UP_ROWS, CHUNK), BF16),
            pltpu.VMEM((2, HALF, CHUNK), BF16),
            pltpu.VMEM((2, UP_ROWS, CHUNK), BF16),
            pltpu.VMEM((2, CELLS, CHUNK), BF16),
            pltpu.SemaphoreType.DMA((9,)),
            pltpu.SemaphoreType.DMA((n_cand,)),
            pltpu.SemaphoreType.DMA((n_cand,)),
            pltpu.SemaphoreType.DMA((3, 2, X)),
            pltpu.SemaphoreType.DMA((2, 3, X)),
            pltpu.VMEM((CELLS, C), F32),
            pltpu.VMEM((CELLS + 4 * H, C), BF16),
            pltpu.VMEM((8, C), BF16),
            pltpu.VMEM((H, C), BF16),
            pltpu.VMEM((H, H, C), BF16),
            pltpu.SemaphoreType.DMA((2,)),
            pltpu.SemaphoreType.DMA((H,)),
            pltpu.SemaphoreType.DMA((H,)),
        ],
        compiler_params=pltpu.CompilerParams(
            collective_id=0, has_side_effects=True, vmem_limit_bytes=56 * 1024 * 1024
        ),
        name="step",
    )(
        first_maps,
        layer_of,
        expand_half,
        radius,
        teach_up,
        jnp.transpose(teach_dw, (1, 0, 2)),
        teach_down,
        cand_up,
        jnp.transpose(cand_dw, (1, 0, 2)),
        cand_down,
    )
    up, dw, down = pl.pallas_call(
        finish,
        out_shape=(
            jax.ShapeDtypeStruct((own, 1, C), F32),
            jax.ShapeDtypeStruct((25, 1, own), F32),
            jax.ShapeDtypeStruct((own, 1, C), F32),
        ),
        in_specs=[hbm] * 3,
        out_specs=(vmem, vmem, vmem),
        scratch_shapes=[
            pltpu.VMEM((384, 384), F32),
            pltpu.VMEM((32, 384), F32),
            pltpu.VMEM((384, 384), F32),
            pltpu.SemaphoreType.DMA((3,)),
        ],
        compiler_params=pltpu.CompilerParams(vmem_limit_bytes=60 * 1024 * 1024),
        name="finish",
    )(*grads)
    return (
        jnp.transpose(up, (1, 2, 0)),
        jnp.transpose(dw, (1, 0, 2)),
        jnp.transpose(down, (1, 2, 0)),
    )


def solution(mesh):
    placed = (
        P("img", "cand", None),
        P("cand"),
        P("cand"),
        P("cand"),
        P(),
        P(),
        P(),
        P("cand", None, None),
        P("cand", None, None),
        P("cand", None, None),
    )
    return jax.shard_map(
        functools.partial(body, mesh.shape["cand"], mesh.shape["img"]),
        mesh=mesh,
        in_specs=placed,
        out_specs=(P("cand", None, "img"), P("cand", None, "img"), P("cand", None, "img")),
        check_vma=False,
    )
```

```python
import functools

import jax
import jax.numpy as jnp
from jax import lax
from jax.experimental import pallas as pl
from jax.experimental.pallas import tpu as pltpu
from jax.sharding import PartitionSpec as P

C = 344
HID = 2064
H = 16
CELLS = 256
CHUNK = 256
FULL = HID // CHUNK
REST = HID - FULL * CHUNK
TILES = 2 * FULL + 1
X = 4
DOWN_ROWS = 384
UP_ROWS = 416
PLACES = 1914
ROW_STEP = 4
SIDES = 166
HALF = DOWN_ROWS // 2
INNER = (6, 7, 8, 11, 12, 13, 16, 17, 18)
F32 = jnp.float32
BF16 = jnp.bfloat16
MESH = pl.DeviceIdType.MESH


def sigmoid(v):
    return 0.5 * jnp.tanh(0.5 * v) + 0.5


def shift_columns(grid, b, col):
    if b == 0:
        return grid
    flat = pltpu.roll(grid.reshape(CELLS, 128), (-b) % CELLS, 0)
    moved = flat.reshape(H, H, 128)
    keep = col < H - b if b > 0 else col >= -b
    return jnp.where(keep, moved, 0.0)


def depthwise(e, tap):
    col = lax.broadcasted_iota(jnp.int32, (H, H, 128), 1)
    grid = e.reshape(H, H, 128)
    zero = jnp.zeros((2, H, 128), F32)
    total = None
    for b in range(-2, 3):
        moved = jnp.concatenate([zero, shift_columns(grid, b, col), zero], 0)
        for a in range(5):
            term = tap(5 * a + b + 2)[None, None, :] * moved[a : a + H]
            total = term if total is None else total + term
    return total.reshape(CELLS, 128)


def depthwise_row(e, tap):
    col = lax.broadcasted_iota(jnp.int32, (5, H, 128), 1)
    total = None
    for b in range(-2, 3):
        if b == 0:
            moved = e.reshape(5, H, 128)
        else:
            moved = pltpu.roll(e, (-b) % (5 * H), 0).reshape(5, H, 128)
            moved = jnp.where(col < H - b if b > 0 else col >= -b, moved, 0.0)
        for a in range(5):
            term = tap(5 * a + b + 2)[None, :] * moved[a]
            total = term if total is None else total + term
    return total


def finish(gu_hbm, gk_hbm, gd_hbm, up_ref, dw_ref, down_ref, gu, gk, gd, sem):
    own = CHUNK + 2
    copies = [
        pltpu.make_async_copy(src, dst, sem.at[k])
        for k, (src, dst) in enumerate(((gu_hbm, gu), (gk_hbm, gk), (gd_hbm, gd)))
    ]
    for copy in copies:
        copy.start()
    copies[0].wait()
    up_ref[:, 0, :] = jnp.transpose(gu[...])[:own, :C]
    copies[1].wait()
    dw_ref[:, 0, :] = gk[:25, :own]
    copies[2].wait()
    down_ref[:, 0, :] = jnp.transpose(gd[...])[:own, :C]


def kernel(
    n_cand,
    n_img,
    x_ref,
    layer_ref,
    expand_ref,
    radius_ref,
    tu_hbm,
    tk_hbm,
    td_hbm,
    cu_hbm,
    ck_hbm,
    cd_hbm,
    gu_ref,
    gk_ref,
    gd_ref,
    tu,
    tk,
    td,
    cu,
    ck,
    cd,
    left_u,
    left_d,
    left_k,
    xg,
    x0,
    xb,
    xt,
    acc,
    acc2,
    eb,
    ebt,
    e_s,
    sp_s,
    sk_s,
    g_s,
    p_s,
    rows,
    kg,
    down_own,
    down_y,
    down_sum,
    down_x,
    up_own,
    up_x,
    up_sum,
    up_y,
    down_relay,
    up_relay,
    g_t,
    w_sem,
    xs_sem,
    xr_sem,
    down_sem,
    up_sem,
    base,
    xpad,
    xh,
    row_out,
    row_in,
    pair_sem,
    ts_sem,
    tr_sem,
):
    me_c = lax.axis_index("cand")
    me_i = lax.axis_index("img")

    copies = []
    for layer in range(2):
        for src, dst in ((tu_hbm, tu), (td_hbm, td)):
            copies.append(pltpu.make_async_copy(src.at[layer], dst.at[layer], w_sem.at[len(copies)]))
    copies.insert(0, pltpu.make_async_copy(tk_hbm, tk, w_sem.at[len(copies)]))
    for src, dst in ((cu_hbm.at[0], cu), (ck_hbm, ck), (cd_hbm.at[0], cd)):
        copies.append(pltpu.make_async_copy(src, dst, w_sem.at[len(copies)]))
    for copy in copies:
        copy.start()

    xh[...] = x_ref[0].astype(BF16)
    barrier = pltpu.get_barrier_semaphore()

    def greet_cand(k, carry):
        peer = lax.rem(me_c + k, n_cand)
        pl.semaphore_signal(barrier, inc=1, device_id={"cand": peer}, device_id_type=MESH)
        return carry

    def greet_img(k, carry):
        peer = lax.rem(me_i + k, n_img)
        pl.semaphore_signal(barrier, inc=1, device_id={"img": peer}, device_id_type=MESH)
        return carry

    lax.fori_loop(1, n_cand, greet_cand, 0)
    lax.fori_loop(1, n_img, greet_img, 0)
    pl.semaphore_wait(barrier, n_cand + n_img - 2)

    def map_copy(k):
        peer = lax.rem(me_c + k, n_cand)
        return pltpu.make_async_remote_copy(
            src_ref=xh,
            dst_ref=xg.at[me_c],
            send_sem=xs_sem.at[k],
            recv_sem=xr_sem.at[me_c],
            device_id={"cand": peer},
            device_id_type=MESH,
        )

    def map_arrival(k):
        source = lax.rem(me_c + k, n_cand)
        return pltpu.make_async_remote_copy(
            src_ref=xh,
            dst_ref=xg.at[source],
            send_sem=xs_sem.at[k],
            recv_sem=xr_sem.at[source],
            device_id={"cand": source},
            device_id_type=MESH,
        )

    def start_map(k, carry):
        map_copy(k).start()
        return carry

    def wait_map(k, carry):
        map_arrival(k).wait_recv()
        return carry

    def wait_sent(k, carry):
        map_copy(k).wait_send()
        return carry

    lax.fori_loop(1, n_cand, start_map, 0)
    xg[me_c] = xh[...]

    rows[...] = jnp.zeros_like(rows)
    xpad[...] = jnp.zeros_like(xpad)
    kg[...] = jnp.zeros_like(kg)
    left_u[...] = jnp.zeros_like(left_u)
    left_d[...] = jnp.zeros_like(left_d)
    left_k[...] = jnp.zeros_like(left_k)

    layer_here = layer_ref[0]
    units_used = expand_ref[0] * (HID // 2)
    outer = jnp.where(radius_ref[0] >= 2, 1.0, 0.0).astype(F32)

    def tap_mask(shape):
        row = lax.broadcasted_iota(jnp.int32, shape, 0)
        inner = row == INNER[0]
        for other in INNER[1:]:
            inner = inner | (row == other)
        return jnp.where(inner, 1.0, outer)

    def unit_mask(tile):
        unit = lax.broadcasted_iota(jnp.int32, (1, 128), 1) + tile * 128
        return jnp.where(unit < units_used, 1.0, 0.0)

    def border_mask():
        place = lax.broadcasted_iota(jnp.int32, (1, 128), 1)
        unit = ((place >> 4) + 1) * CHUNK + (place & 15)
        return jnp.where(unit < units_used, 1.0, 0.0)

    def lanes(j):
        return pl.ds(pl.multiple_of(j * CHUNK, CHUNK), CHUNK)

    def tile_lanes(tile):
        return pl.ds(pl.multiple_of(tile * 128, 128), 128)

    def active(p, conv):
        k = conv(p * sigmoid(p))
        return (k * sigmoid(k)).astype(BF16)

    def whole_map(tap):
        return lambda e: depthwise(e, tap)

    def one_row(tap):
        return lambda e: depthwise_row(e, tap)

    def load_left(layer):
        left_u[layer, :, :REST] = tu[layer, :, FULL * CHUNK :]
        left_d[layer, :, :REST] = td[layer, :, FULL * CHUNK :]
        left_k[layer, :25, :REST] = tk[:, layer, FULL * CHUNK :]

    core = lax.rem(me_c, 2)
    map_row = me_c // 2

    def teacher_first():
        p = jnp.dot(xb[...], left_u[0], preferred_element_type=F32)
        g = active(p, whole_map(lambda i: left_k[0, i, :]))
        rest = lax.dot_general(g, left_d[0], (((1,), (1,)), ((), ())), preferred_element_type=F32)
        acc[...] = jnp.where(core == 0, rest, 0.0)

        def step(t, carry):
            j = core * (FULL // 2) + t
            p_s[0] = jnp.dot(xb[...], tu[0, :, lanes(j)], preferred_element_type=F32)
            for half in range(2):
                part = slice(128 * half, 128 * half + 128)
                tile = 2 * j + half
                g_s[FULL, :, part] = active(
                    p_s[0, :, part], whole_map(lambda i: tk[i, 0, tile_lanes(tile)])
                )
            acc[...] += lax.dot_general(
                g_s[FULL], td[0, :, lanes(j)], (((1,), (1,)), ((), ())), preferred_element_type=F32
            )
            return carry

        lax.fori_loop(0, FULL // 2, step, 0)

    def pair_copy():
        return pltpu.make_async_remote_copy(
            src_ref=acc,
            dst_ref=acc2,
            send_sem=pair_sem.at[0],
            recv_sem=pair_sem.at[1],
            device_id={"cand": me_c + 1 - 2 * core},
            device_id_type=MESH,
        )

    def teacher_row():
        near = xpad[pl.ds(pl.multiple_of(map_row * H, H), 5 * H), :]
        p = jnp.dot(near, left_u[1], preferred_element_type=F32)
        g = active(p, one_row(lambda i: left_k[1, i, :]))
        rest = lax.dot_general(g, left_d[1], (((1,), (1,)), ((), ())), preferred_element_type=F32)

        def step(m, total):
            for k in range(ROW_STEP):
                j = ROW_STEP * m + k
                p = jnp.dot(near, tu[1, :, lanes(j)], preferred_element_type=F32)
                parts = []
                for half in range(2):
                    tile = 2 * j + half
                    parts.append(
                        active(
                            p[:, 128 * half : 128 * half + 128],
                            one_row(lambda i, tile=tile: tk[i, 1, tile_lanes(tile)]),
                        )
                    )
                total = total + lax.dot_general(
                    jnp.concatenate(parts, 1),
                    td[1, :, lanes(j)],
                    (((1,), (1,)), ((), ())),
                    preferred_element_type=F32,
                )
            return total

        row_out[...] = lax.fori_loop(0, FULL // ROW_STEP, step, rest).astype(BF16)

    def row_copy(k):
        peer = lax.rem(me_c + 2 * k, n_cand)
        return pltpu.make_async_remote_copy(
            src_ref=row_out,
            dst_ref=row_in.at[map_row],
            send_sem=ts_sem.at[k],
            recv_sem=tr_sem.at[map_row],
            device_id={"cand": peer},
            device_id_type=MESH,
        )

    def row_arrival(k):
        source = lax.rem(map_row + k, H)
        return pltpu.make_async_remote_copy(
            src_ref=row_out,
            dst_ref=row_in.at[source],
            send_sem=ts_sem.at[k],
            recv_sem=tr_sem.at[source],
            device_id={"cand": lax.rem(me_c + 2 * k, n_cand)},
            device_id_type=MESH,
        )

    def start_row(k, carry):
        row_copy(k).start()
        return carry

    def wait_row(k, carry):
        row_arrival(k).wait_recv()
        return carry

    def sent_row(k, carry):
        row_copy(k).wait_send()
        return carry

    for copy in copies:
        copy.wait()
    load_left(0)
    load_left(1)
    ck[...] = ck[...] * tap_mask((25, 1, HID))
    lane = lax.broadcasted_iota(jnp.int32, (1, 128), 1)

    def borders(block, rows_of):
        whole = jnp.zeros((rows_of, 128), F32)
        for k in range(n_img):
            part = block(k + 1).astype(F32)
            part = part if k == 0 else pltpu.roll(part, REST * k, 1)
            whole = jnp.where((lane >> 4) == k, part, whole)
        return whole

    def wide_tile(ref, k):
        if k == FULL:
            return jnp.concatenate([ref[:, FULL * CHUNK :], jnp.zeros((C, 128 - REST), BF16)], 1)
        return ref[:, k * CHUNK : k * CHUNK + 128]

    def tap_tile(k):
        if k == FULL:
            return jnp.concatenate(
                [ck[:, 0, FULL * CHUNK :], jnp.zeros((25, 128 - REST), F32)], 1
            )
        return ck[:, 0, k * CHUNK : k * CHUNK + 128]

    left_u[2] = borders(lambda k: wide_tile(cu, k), C).astype(BF16)
    edge_down = borders(lambda k: wide_tile(cd, k), C)
    left_d[2] = edge_down.astype(BF16)
    left_d[3] = jnp.where(lane >= 128 - REST, edge_down, 0.0).astype(BF16)
    left_k[2, :25] = borders(tap_tile, 25)

    lax.fori_loop(1, n_cand, wait_map, 0)
    x_wide = xg[...].astype(F32).reshape(CELLS, C)
    x0[...] = x_wide
    xb[...] = x_wide.astype(BF16)
    teacher_first()
    pair = pair_copy()
    pair.start()
    pair.wait()
    ones = x0[...] + (acc[...] + acc2[...])
    base[...] = acc[...] + acc2[...]
    xpad[2 * H : 2 * H + CELLS] = ones.astype(BF16)
    teacher_row()
    lax.fori_loop(1, H, start_row, 0)
    row_in[map_row] = row_out[...]
    first = layer_here == 0
    wide = jnp.where(first, x0[...], ones)
    xb[...] = wide.astype(BF16)
    pad = jnp.zeros((CELLS, 384 - C), F32)
    xt[...] = jnp.transpose(jnp.concatenate([wide, pad], 1))[:C].astype(BF16)

    def forward_tile(p, tile, tap, mask):
        s = sigmoid(p) * mask
        e = p * s
        e_s[tile] = e
        sp_s[tile] = s + e * (1.0 - s)
        k = depthwise(e, tap)
        s2 = sigmoid(k)
        g = k * s2
        sk_s[tile] = s2 + g * (1.0 - s2)
        return g.astype(BF16)

    p = jnp.dot(xb[...], left_u[2], preferred_element_type=F32)
    g = forward_tile(p, 2 * FULL, lambda i: left_k[2, i, :], border_mask())
    g_s[FULL, :, :128] = g
    acc2[...] = lax.dot_general(g, left_d[3], (((1,), (1,)), ((), ())), preferred_element_type=F32)

    def up_product(j, slot):
        p_s[slot] = jnp.dot(xb[...], cu[:, lanes(j)], preferred_element_type=F32)

    def forward(m, carry):
        for slot in range(2):
            j = 2 * m + slot
            up_product(lax.rem(j + 1, FULL), 1 - slot)
            for half in range(2):
                part = slice(128 * half, 128 * half + 128)
                tile = 2 * j + half
                g = forward_tile(
                    p_s[slot, :, part],
                    tile,
                    lambda i, tile=tile: ck[i, 0, tile_lanes(tile)],
                    unit_mask(tile),
                )
                g_t[slot, :, part] = g
                g_s[j, :, part] = g
            acc2[...] += lax.dot_general(
                g_t[slot], cd[:, lanes(j)], (((1,), (1,)), ((), ())), preferred_element_type=F32
            )
        return carry

    up_product(0, 0)
    lax.fori_loop(0, FULL // 2, forward, 0)

    lax.fori_loop(1, H, wait_row, 0)
    second = row_in[...].astype(F32).reshape(CELLS, C)
    error = (acc2[...] - jnp.where(first, base[...], second)) * (1.0 / n_img)
    eb[...] = error.astype(BF16)
    ebt[...] = jnp.transpose(jnp.concatenate([error, pad], 1))[:C].astype(BF16)

    my_x = lax.rem(me_i, X)
    my_y = me_i // X

    def send(src, dst, sems, peer):
        return pltpu.make_async_remote_copy(
            src_ref=src,
            dst_ref=dst,
            send_sem=sems[0],
            recv_sem=sems[1],
            device_id={"img": peer},
            device_id_type=MESH,
        )

    def down_over_y(x):
        slab = X * (1 - my_y) + x
        return send(
            down_own.at[slab],
            down_y.at[x],
            (down_sem.at[0, 0, x], down_sem.at[0, 1, x]),
            X * (1 - my_y) + my_x,
        )

    def down_over_x(x, source):
        return send(
            down_sum.at[x],
            down_x.at[source],
            (down_sem.at[1, 0, x], down_sem.at[1, 1, source]),
            X * my_y + x,
        )

    def up_over_x(y, x, source):
        return send(
            up_own.at[X * y + x],
            up_x.at[y, source],
            (up_sem.at[0, y, x], up_sem.at[1, y, source]),
            X * my_y + x,
        )

    def side(h):
        return lax.rem(1 - my_y + h, 2)

    def opposite(h):
        return lax.rem(my_x + 3 - 2 * h, X)

    def down_half(h):
        return send(
            down_sum.at[lax.rem(my_x + 2, X), pl.ds(HALF * h, HALF)],
            down_relay.at[h],
            (down_sem.at[2, 0, h], down_sem.at[2, 1, h]),
            X * my_y + opposite(h),
        )

    def up_half(h):
        return send(
            up_own.at[X * side(h) + lax.rem(my_x + 2, X)],
            up_relay.at[h],
            (up_sem.at[0, 2, 1 + h], up_sem.at[1, 2, 1 + h]),
            X * my_y + opposite(h),
        )

    def up_over_y():
        return send(
            up_sum, up_y, (up_sem.at[0, 2, 0], up_sem.at[1, 2, 0]), X * (1 - my_y) + my_x
        )

    def turn(block, other):
        return jnp.dot(
            jnp.transpose(block).astype(BF16), other, preferred_element_type=F32
        ).astype(BF16)

    def place_heads(ref, heads):
        for k in range(n_img):
            part = slice(REST * k, REST * k + REST)
            ref[k, 352:368, :] = heads[part, :CHUNK]
            ref[k, 368:384, : C - CHUNK] = heads[part, CHUNK:]

    place_heads(down_own, turn(g_s[FULL, :, :128].astype(F32), eb[...]))

    def down_slab(y, x):
        j = X * y + x
        down_own[j, :C] = jnp.dot(ebt[...], g_s[j], preferred_element_type=F32).astype(BF16)

    def start_down(k):
        x = lax.rem(my_x + k, X)
        down_slab(1 - my_y, x)
        down_over_y(x).start()

    start_down(2)

    def relay_down(x):
        j = X * my_y + x
        down_over_y(x).wait_recv()
        own = jnp.dot(ebt[...], g_s[j], preferred_element_type=F32)
        down_sum[x, :C] = (own + down_y[x, :C].astype(F32)).astype(BF16)
        down_sum[x, 352:] = (
            down_own[j, 352:].astype(F32) + down_y[x, 352:].astype(F32)
        ).astype(BF16)

    def split_down():
        relay_down(lax.rem(my_x + 2, X))
        for h in range(2):
            down_half(h).start()

    def join_down(h):
        x = opposite(h)
        relay_down(x)
        down_half(h).wait_recv()
        part = slice(HALF * h, HALF * h + HALF)
        down_sum[x, part] = (
            down_sum[x, part].astype(F32) + down_relay[h].astype(F32)
        ).astype(BF16)
        down_over_x(x, my_x).start()

    def backward_tile(dg, tile, tap):
        col = lax.broadcasted_iota(jnp.int32, (H, H, 128), 1)
        grid = (dg * sk_s[tile]).reshape(H, H, 128)
        for b in range(-2, 3):
            rows[b + 2, 2 : 2 + H] = shift_columns(grid, -b, col)
        total = [None] * H
        for b in range(-2, 3):
            sums = [None] * 5
            for r in range(H):
                e = e_s[tile, H * r : H * r + H, :]
                for a in range(-2, 3):
                    moved = rows[b + 2, 2 - a + r]
                    term = tap(5 * (a + 2) + b + 2)[None, :] * moved
                    total[r] = term if total[r] is None else total[r] + term
                    q = moved * e
                    q = q[:8] + q[8:]
                    sums[a + 2] = q if sums[a + 2] is None else sums[a + 2] + q
            for a in range(5):
                kg[5 * a + b + 2, :] = jnp.sum(sums[a], axis=0)
        de = jnp.concatenate(total, 0)
        return de * sp_s[tile]

    taps = tap_mask((32, 128))

    dg = jnp.dot(eb[...], left_d[2], preferred_element_type=F32)
    dp = backward_tile(dg, 2 * FULL, lambda i: left_k[2, i, :])
    place_heads(up_own, turn(dp, xb[...]))
    edge = kg[...] * taps
    for k in range(n_img):
        moved = edge if k == 0 else pltpu.roll(edge, 128 - REST * k, 1)
        low = jnp.where(lane < REST, moved[:REST], pltpu.roll(moved[REST:], REST, 1))
        up_own[k, 368:384, 128:] = low.astype(BF16)

    def up_step(t, carry):
        k = (jnp.int32(PLACES) >> (2 * t)) & 3
        x = lax.rem(my_x + k, X)
        y = side((jnp.int32(SIDES) >> t) & 1)
        j = X * y + x
        p_s[0] = jnp.dot(eb[...], cd[:, lanes(j)], preferred_element_type=F32)
        for half in range(2):
            part = slice(128 * half, 128 * half + 128)
            tile = 2 * j + half
            p_s[0, :, part] = backward_tile(
                p_s[0, :, part], tile, lambda i: ck[i, 0, tile_lanes(tile)]
            )
            up_own[j, 384:416, part] = (kg[...] * taps).astype(BF16)
        up_own[j, :C] = jnp.dot(
            xt[...], p_s[0].astype(BF16), preferred_element_type=F32
        ).astype(BF16)

        @pl.when(t < 2)
        def _():
            up_half(t).start()

        for when, which in ((0, 3), (1, 1), (2, 0)):

            @pl.when(t == when)
            def _():
                start_down(which)

        @pl.when((t == 4) | (t == 5))
        def _():
            h = t - 4
            up_half(h).wait_recv()
            up_own[j] = (up_own[j].astype(F32) + up_relay[h].astype(F32)).astype(BF16)

        @pl.when((t >= 2) & (t < 6))
        def _():
            up_over_x(y, x, my_x).start()

        @pl.when(t == 2)
        def _():
            split_down()

        @pl.when(t == 6)
        def _():
            join_down(0)

        return carry

    lax.fori_loop(0, n_img, up_step, 0)
    join_down(1)

    def sum_x(y):
        total = up_own[X * y + my_x].astype(F32)
        for k in (1, 3):
            source = lax.rem(my_x + k, X)
            up_over_x(y, source, source).wait_recv()
            total = total + up_x[y, source].astype(F32)
        return total

    up_sum[...] = sum_x(1 - my_y).astype(BF16)
    up_over_y().start()
    relay_down(my_x)

    amount = lax.rem(384 - 2 * me_i, 384)
    wide_zero = jnp.zeros((128 - REST, 384), F32)
    lane_zero = jnp.zeros((REST, 384 - C), F32)

    def assemble(total, out):
        heads = jnp.concatenate([total[352:368], total[368:384, : C - CHUNK], lane_zero], 1)
        tail = jnp.transpose(jnp.concatenate([heads, wide_zero], 0))[:C]
        out[:C, :] = pltpu.roll(jnp.concatenate([total[:C], tail], 1), amount, 1)
        out[C:, :] = jnp.zeros((384 - C, 384), F32)

    total = down_sum[my_x].astype(F32)
    for k in (1, 3):
        source = lax.rem(my_x + k, X)
        down_over_x(source, source).wait_recv()
        total = total + down_x[source].astype(F32)
    assemble(total, gd_ref)

    total = sum_x(my_y)
    up_over_y().wait_recv()
    total = total + up_y[...].astype(F32)
    assemble(total, gu_ref)
    low = total[368:384, 128:]
    edge = jnp.concatenate([low, pltpu.roll(low, 128 - REST, 1)], 0)
    gk_ref[...] = pltpu.roll(
        jnp.concatenate([total[384:416], edge], 1), amount, 1
    )

    lax.fori_loop(1, n_cand, wait_sent, 0)
    lax.fori_loop(1, H, sent_row, 0)

    def sent_y(x, carry):
        down_over_y(x).wait_send()
        return carry

    lax.fori_loop(0, X, sent_y, 0)

    for k in (1, 3):
        x = lax.rem(my_x + k, X)
        down_over_x(x, my_x).wait_send()
        up_over_x(0, x, my_x).wait_send()
        up_over_x(1, x, my_x).wait_send()
    for h in range(2):
        down_half(h).wait_send()
        up_half(h).wait_send()
    up_over_y().wait_send()


def body(n_cand, n_img, first_maps, layer_of, expand_half, radius, *weights):
    teach_up, teach_dw, teach_down, cand_up, cand_dw, cand_down = weights
    vmem = pl.BlockSpec(memory_space=pltpu.VMEM)
    smem = pl.BlockSpec(memory_space=pltpu.SMEM)
    hbm = pl.BlockSpec(memory_space=pl.ANY)
    own = CHUNK + 2
    grads = pl.pallas_call(
        functools.partial(kernel, n_cand, n_img),
        out_shape=(
            jax.ShapeDtypeStruct((384, 384), F32),
            jax.ShapeDtypeStruct((32, 384), F32),
            jax.ShapeDtypeStruct((384, 384), F32),
        ),
        in_specs=[vmem, smem, smem, smem] + [hbm] * 6,
        out_specs=(vmem, vmem, vmem),
        scratch_shapes=[
            pltpu.VMEM((2, C, HID), BF16),
            pltpu.VMEM((25, 2, HID), F32),
            pltpu.VMEM((2, C, HID), BF16),
            pltpu.VMEM((C, HID), BF16),
            pltpu.VMEM((25, 1, HID), F32),
            pltpu.VMEM((C, HID), BF16),
            pltpu.VMEM((3, C, 128), BF16),
            pltpu.VMEM((4, C, 128), BF16),
            pltpu.VMEM((3, 32, 128), F32),
            pltpu.VMEM((n_cand, 8, C), BF16),
            pltpu.VMEM((CELLS, C), F32),
            pltpu.VMEM((CELLS, C), BF16),
            pltpu.VMEM((C, CELLS), BF16),
            pltpu.VMEM((CELLS, C), F32),
            pltpu.VMEM((CELLS, C), F32),
            pltpu.VMEM((CELLS, C), BF16),
            pltpu.VMEM((C, CELLS), BF16),
            pltpu.VMEM((TILES, CELLS, 128), F32),
            pltpu.VMEM((TILES, CELLS, 128), F32),
            pltpu.VMEM((TILES, CELLS, 128), F32),
            pltpu.VMEM((FULL + 1, CELLS, CHUNK), BF16),
            pltpu.VMEM((2, CELLS, CHUNK), F32),
            pltpu.VMEM((5, H + 4, H, 128), F32),
            pltpu.VMEM((32, 128), F32),
            pltpu.VMEM((n_img, DOWN_ROWS, CHUNK), BF16),
            pltpu.VMEM((X, DOWN_ROWS, CHUNK), BF16),
            pltpu.VMEM((X, DOWN_ROWS, CHUNK), BF16),
            pltpu.VMEM((X, DOWN_ROWS, CHUNK), BF16),
            pltpu.VMEM((n_img, UP_ROWS, CHUNK), BF16),
            pltpu.VMEM((2, X, UP_ROWS, CHUNK), BF16),
            pltpu.VMEM((UP_ROWS, CHUNK), BF16),
            pltpu.VMEM((UP_ROWS, CHUNK), BF16),
            pltpu.VMEM((2, HALF, CHUNK), BF16),
            pltpu.VMEM((2, UP_ROWS, CHUNK), BF16),
            pltpu.VMEM((2, CELLS, CHUNK), BF16),
            pltpu.SemaphoreType.DMA((9,)),
            pltpu.SemaphoreType.DMA((n_cand,)),
            pltpu.SemaphoreType.DMA((n_cand,)),
            pltpu.SemaphoreType.DMA((3, 2, X)),
            pltpu.SemaphoreType.DMA((2, 3, X)),
            pltpu.VMEM((CELLS, C), F32),
            pltpu.VMEM((CELLS + 4 * H, C), BF16),
            pltpu.VMEM((8, C), BF16),
            pltpu.VMEM((H, C), BF16),
            pltpu.VMEM((H, H, C), BF16),
            pltpu.SemaphoreType.DMA((2,)),
            pltpu.SemaphoreType.DMA((H,)),
            pltpu.SemaphoreType.DMA((H,)),
        ],
        compiler_params=pltpu.CompilerParams(
            collective_id=0, has_side_effects=True, vmem_limit_bytes=56 * 1024 * 1024
        ),
        name="step",
    )(
        first_maps,
        layer_of,
        expand_half,
        radius,
        teach_up,
        jnp.transpose(teach_dw, (1, 0, 2)),
        teach_down,
        cand_up,
        jnp.transpose(cand_dw, (1, 0, 2)),
        cand_down,
    )
    up, dw, down = pl.pallas_call(
        finish,
        out_shape=(
            jax.ShapeDtypeStruct((own, 1, C), F32),
            jax.ShapeDtypeStruct((25, 1, own), F32),
            jax.ShapeDtypeStruct((own, 1, C), F32),
        ),
        in_specs=[hbm] * 3,
        out_specs=(vmem, vmem, vmem),
        scratch_shapes=[
            pltpu.VMEM((384, 384), F32),
            pltpu.VMEM((32, 384), F32),
            pltpu.VMEM((384, 384), F32),
            pltpu.SemaphoreType.DMA((3,)),
        ],
        compiler_params=pltpu.CompilerParams(vmem_limit_bytes=60 * 1024 * 1024),
        name="finish",
    )(*grads)
    return (
        jnp.transpose(up, (1, 2, 0)),
        jnp.transpose(dw, (1, 0, 2)),
        jnp.transpose(down, (1, 2, 0)),
    )


def solution(mesh):
    placed = (
        P("img", "cand", None),
        P("cand"),
        P("cand"),
        P("cand"),
        P(),
        P(),
        P(),
        P("cand", None, None),
        P("cand", None, None),
        P("cand", None, None),
    )
    return jax.shard_map(
        functools.partial(body, mesh.shape["cand"], mesh.shape["img"]),
        mesh=mesh,
        in_specs=placed,
        out_specs=(P("cand", None, "img"), P("cand", None, "img"), P("cand", None, "img")),
        check_vma=False,
    )
```
